256 devices in a mesh: dp: 32 (over z, x_hi, core), row: 4 (over y), col: 2 (over x_lo).
Axes of the slice: x: 4 (x_hi: 2, x_lo: 2; x = x_hi * 2 + x_lo), y: 4, z: 8, core: 2. Of those that a mesh axis runs over, the one named last changes fastest.
Arguments:
- tokens: bfloat16 [6144, 4096], P('dp', ('row', 'col')), may hold values from -6 to 6
- in_weight: bfloat16 [4096, 3, 4096], P('dp', None, ('row', 'col')), may hold values from -0.09375 to 0.09375
- short_filter: float32 [3, 3, 4096], P(None, None, ('row', 'col')), may hold values from -3 to 3
- long_filter: bfloat16 [256, 128], P(('row', 'col')), may hold values from -0.59765625 to 0.59765625
- grad_out: bfloat16 [6144, 4096], P('dp', ('row', 'col')), may hold values from -6 to 6
Outputs:
- mixed: bfloat16 [6144, 4096], P('dp', ('row', 'col'))
- grad_in: bfloat16 [6144, 4096], P('dp', ('row', 'col'))
- grad_weight: float32 [4096, 3, 4096], P('dp', None, ('row', 'col'))
- grad_long: float32 [256, 128], P(('row', 'col'))
- grad_short: float32 [3, 3, 4096], P(None, None, ('row', 'col'))
The draws below stay inside these ranges and needn't reach their ends.
All inputs are finite; a program needn't handle non-finite values.
Results may differ from the reference program's by a relative error of at most 0.019.
Values may be sent and summed in bfloat16 or wider, within the bound.
A program may use at most 128 MiB of HBM per device.

```python
import jax
import jax.numpy as jnp
from jax import lax

DIN = 4096
CH = 4096
GROUP = 16
LTAPS = 128
SHORT = 3
TOK_DEV = 192
TOKENS = 6144
GROUPS = 256
N_DP = 32


def strengthened(entries, rng, source, target, shards_of, factor):
    def block_of(axis_at):
        return (jnp.arange(entries.shape[axis_at]) // (entries.shape[axis_at] // shards_of)).reshape((-1,) + (1,) * (entries.ndim - 1 - axis_at))

    first = jax.random.permutation(rng, shards_of)[block_of(target)]
    other_side = (block_of(target) + shards_of // 2) % shards_of
    return jnp.where((block_of(source) == first) | (block_of(source) == other_side), factor * entries, entries)


def steps_of(own_key, dims, split, smallest, high):
    def one(axis_at, blocks):
        draws = jax.random.uniform(jax.random.fold_in(jax.random.fold_in(own_key, 6), axis_at), (blocks,), jnp.float32, smallest / len(split), high / len(split))
        return jnp.repeat(jnp.exp(draws), dims[axis_at] // blocks).reshape((-1,) + (1,) * (len(dims) - axis_at - 1))

    level = one(*split[0])
    for cut in split[1:]:
        level = level * one(*cut)
    return level


def noise(stream_key, extent, spread, limit, cuts=(), kind=jnp.bfloat16):
    drawn = spread * jax.random.normal(stream_key, extent, jnp.float32)
    if cuts:
        drawn = drawn * steps_of(stream_key, extent, cuts, -0.22, 0.18)
    return jnp.clip(drawn, -limit, limit).astype(kind)


def gaussian_with(own_key, dims, spread, most, cuts, heavy, kind=jnp.bfloat16):
    values = spread * jax.random.normal(own_key, dims, jnp.float32)
    if cuts:
        values = values * steps_of(own_key, dims, cuts, -0.22, 0.18)
    return jnp.clip(strengthened(values, jax.random.fold_in(own_key, 3), *heavy), -most, most).astype(kind)


def setup_inputs(seed: int = 0) -> dict:
    streams_of = jax.random.split(jax.random.key(seed), 6)
    tokens = gaussian_with(streams_of[0], (TOKENS, DIN), 1.0, 6.0, ((0, 32), (1, 8)), (0, 1, 32, 2.75))
    in_weight = noise(streams_of[1], (DIN, 3, CH), DIN ** -0.5, 0.09375, ((0, 32), (2, 8)))
    short_filter = noise(streams_of[2], (SHORT, 3, CH), 0.5, 3.0, ((2, 8),), jnp.float32)
    long_filter = noise(streams_of[3], (GROUPS, LTAPS), 0.1, 0.59765625, ((0, 8),))
    grad_out = noise(streams_of[4], (TOKENS, CH), 1.0, 6.0, ((0, 32), (1, 8)))
    return {"tokens": tokens, "in_weight": in_weight, "short_filter": short_filter, "long_filter": long_filter, "grad_out": grad_out}


def reference(tokens, in_weight, short_filter, long_filter, grad_out):
    scale = float(TOKENS) ** -0.5
    flat_w = in_weight.reshape(DIN, 3 * CH)
    mixed_in = jnp.dot(tokens, flat_w, preferred_element_type=jnp.float32).astype(jnp.bfloat16).reshape(TOKENS, 3, CH)
    lead = SHORT - 1
    padded = jnp.pad(mixed_in.astype(jnp.float32), ((lead, 0), (0, 0), (0, 0)))
    feats = jnp.zeros((TOKENS, 3, CH), jnp.float32)
    for j in range(SHORT):
        feats = feats + short_filter[j][None] * padded[lead - j: lead - j + TOKENS]
    product = (feats[:, 1] * feats[:, 2]).astype(jnp.bfloat16)
    taps = jnp.repeat(long_filter.astype(jnp.float32), GROUP, axis=0)
    margin = LTAPS - 1
    prod_pad = jnp.pad(product.astype(jnp.float32), ((margin, 0), (0, 0)))

    def tap_column(j):
        return lax.dynamic_slice_in_dim(taps, j.astype(jnp.int32), 1, 1).reshape(1, CH)

    def conv_step(j, total):
        start = (margin - j).astype(jnp.int32)
        piece = lax.dynamic_slice_in_dim(prod_pad, start, TOKENS, 0)
        return total + tap_column(j) * piece

    conv = lax.fori_loop(0, LTAPS, conv_step, jnp.zeros((TOKENS, CH), jnp.float32))
    mixed = (feats[:, 0] * conv).astype(jnp.bfloat16)

    upstream = grad_out.astype(jnp.float32)
    grad_query = upstream * conv
    grad_conv = (upstream * feats[:, 0]).astype(jnp.bfloat16)
    grad_conv32 = grad_conv.astype(jnp.float32)
    grad_pad = jnp.pad(grad_conv32, ((0, margin), (0, 0)))

    def back_step(j, total):
        piece = lax.dynamic_slice_in_dim(grad_pad, j.astype(jnp.int32), TOKENS, 0)
        return total + tap_column(j) * piece

    grad_product = lax.fori_loop(0, LTAPS, back_step, jnp.zeros((TOKENS, CH), jnp.float32))

    def filter_tap(j):
        start = (margin - j).astype(jnp.int32)
        piece = lax.dynamic_slice_in_dim(prod_pad, start, TOKENS, 0)
        return jnp.sum(grad_conv32 * piece, axis=0).reshape(GROUPS, GROUP).sum(axis=1)

    grad_long = lax.map(filter_tap, jnp.arange(LTAPS, dtype=jnp.int32)).T * scale

    grad_feats = jnp.stack([grad_query, grad_product * feats[:, 2], grad_product * feats[:, 1]], axis=1)
    feats_pad = jnp.pad(grad_feats, ((0, lead), (0, 0), (0, 0)))
    grad_acc = jnp.zeros((TOKENS, 3, CH), jnp.float32)
    for j in range(SHORT):
        grad_acc = grad_acc + short_filter[j][None] * feats_pad[j: j + TOKENS]
    grad_mixed = grad_acc.astype(jnp.bfloat16)
    grad_short = jnp.stack([jnp.sum(grad_feats * padded[lead - j: lead - j + TOKENS], axis=0) for j in range(SHORT)]) * scale

    flat_grad = grad_mixed.reshape(TOKENS, 3 * CH)
    grad_in = jnp.dot(flat_grad, flat_w.T, preferred_element_type=jnp.float32).astype(jnp.bfloat16)

    token_blocks = tokens.reshape(N_DP, TOK_DEV, DIN)
    grad_blocks = flat_grad.reshape(N_DP, TOK_DEV, 3 * CH)

    def add_block(total, pair):
        term = jnp.dot(pair[0].T, pair[1], preferred_element_type=jnp.float32) * scale
        rounded = lax.optimization_barrier(term.astype(jnp.bfloat16))
        return total + rounded.astype(jnp.float32), None

    grad_flat, unused = lax.scan(add_block, jnp.zeros((DIN, 3 * CH), jnp.float32), (token_blocks, grad_blocks))
    grad_weight = grad_flat.reshape(DIN, 3, CH)
    return mixed, grad_in, grad_weight, grad_long, grad_short
```

```python
import jax
import jax.numpy as jnp
from jax import lax
from jax.experimental import pallas as pl
from jax.experimental.pallas import tpu as pltpu
from jax.sharding import PartitionSpec as P

MESH = pl.DeviceIdType.MESH
F32, BF16 = jnp.float32, jnp.bfloat16
SIGNS = (1, -1)
LINK_RATE = {"z": 46.0e3, "x": 46.0e3, "y": 46.0e3, "d": 200.0e3}
LINK_LATENCY = {"z": 1.6, "x": 1.6, "y": 1.6, "d": 1.0}


def planned_order(tasks, msgs):
    arrival, done, link_free = {}, {}, {}
    left, order, now = list(tasks), [], 0.0
    while left:
        best = None
        for at, task in enumerate(left):
            ready = 0.0
            for dep in task["deps"]:
                when = arrival.get(dep, done.get(dep))
                if when is None:
                    ready = None
                    break
                ready = max(ready, when)
            if ready is None:
                continue
            key = (max(ready, now), task["prio"], ready, at)
            if best is None or key < best[0]:
                best = (key, at)
        task = left.pop(best[1])
        now = best[0][0] + task["cost"]
        done[task["name"]] = now
        order.append(task)
        for name in task["sends"]:
            link, nbytes, hops = msgs[name]["link"], msgs[name]["bytes"], msgs[name]["hops"]
            begin = max(now, link_free.get(link, 0.0))
            link_free[link] = begin + nbytes * hops / LINK_RATE[link[0]]
            arrival[name] = link_free[link] + LINK_LATENCY[link[0]] * hops
    return order, now


def block_kernel(
    tokens, w3, sf, lf, gout, mixed_out, gin_out, gw_out, gl_out, gs_out,
    tok, wst, wb, go, acc, mx, gox, toe, voe, lfs, sfs, mxo, mxt, mr, gmt, gm,
    glb, gsb, smv, smr, smt, sqr, gp, ws, wr, fs, fr, pp, pr, q1, h1s, h1, s1, q2, h2s, h2,
    ssem, rsem, *, nz, scale,
):
    dp, y, xl = lax.axis_index("dp"), lax.axis_index("row"), lax.axis_index("col")
    z, r = dp // 4, dp % 4
    xh, c = r // 2, r % 2
    x = xh * 2 + xl
    rows, cols = tokens.shape
    quarter = rows // 4
    ntok = 4 * rows
    ngroups, members = mx.shape[1], mx.shape[2]
    nblocks = ntok // 128
    half_z = nz // 2

    def wrap(value, n):
        return lax.rem(value + 2 * n, n)

    def mate(m):
        other_h = 1 - xh if m & 2 else xh
        other_c = 1 - c if m & 1 else c
        return other_h * 2 + other_c

    def at_z(e):
        return (wrap(z + e, nz) * 4 + r, y, xl)

    def at_quad(m):
        return (z * 4 + mate(m), y, xl)

    def at_xy(axis, d):
        if axis == "y":
            return (dp, wrap(y + d, 4), xl)
        there = wrap(x + d, 4)
        return (z * 4 + (there // 2) * 2 + c, y, there % 2)

    def place(axis, first, second):
        dx, dy = (first, second) if axis == "x" else (second, first)
        px, py = wrap(x + dx, 4), wrap(y + dy, 4)
        return py * 2 + px % 2, px // 2

    msgs, tasks = {}, []

    def msg(name, src, dst, dev, link, nbytes, hops=1):
        msgs[name] = dict(src=src, dst=dst, dev=dev, link=link, bytes=nbytes, hops=hops, index=len(msgs))
        return name

    def task(name, deps=(), run=None, sends=(), cost=0.02, prio=5):
        tasks.append(dict(name=name, deps=list(deps), run=run, sends=list(sends), cost=cost, prio=prio))
        return name

    def copy_of(name):
        m = msgs[name]
        i = m["index"]
        return pltpu.make_async_remote_copy(
            src_ref=m["src"](), dst_ref=m["dst"](), send_sem=ssem.at[i], recv_sem=rsem.at[i],
            device_id=m["dev"](), device_id_type=MESH,
        )

    def lanes(block):
        return pl.ds(pl.multiple_of(block * 128, 128), 128)

    wbytes = 128 * 384 * 2
    for m in (1, 2, 3):
        link, hops = ("d", 1) if m == 1 else ("x+", 2)
        msg(("wq", m), lambda m=m: wst.at[mate(m)], lambda: wb.at[z, r], lambda m=m: at_quad(m), link, wbytes, hops)
        msg(("goq", m), lambda m=m: gout.at[:, lanes(mate(m))], lambda: go.at[r], lambda m=m: at_quad(m), link, rows * 256, hops)
    task("quad_w", sends=[("wq", 1), ("wq", 2), ("wq", 3)], prio=0)
    task("quad_go", deps=["quad_w", "tok_first"], sends=[("goq", 1), ("goq", 2), ("goq", 3)], prio=1)

    def reach(m, d, gather):
        return half_z if (m < 2) == (d > 0) else half_z - 1

    for m in range(4):
        for d in SIGNS:
            for h in range(1, reach(m, d, True) + 1):
                where = lambda m=m, d=d, h=h: wb.at[wrap(z - d * (h - 1), nz), mate(m)]
                name = msg(("w", m, d, h), where, where, lambda d=d: at_z(d), "z+" if d > 0 else "z-", wbytes)
                if h > 1:
                    deps = [("w", m, d, h - 1)]
                else:
                    deps = [("wq", m)] if m else []
                task(("send", name), deps=deps, sends=[name], prio=0 if m < 2 else 1)

    hb, qb = 2 * quarter * cols * 2, quarter * cols * 2
    token_msgs = []
    for h in (0, 1):
        a1, a2 = ("x", "y") if h == 0 else ("y", "x")

        def piece(o, u, part, h=h, a1=a1):
            k, ph = place(a1, o, u)
            begin, size = {0: (0, 2), 1: (0, 1), -1: (1, 1)}[part]
            return tok.at[k, ph * 2 + c, pl.ds(h * 2 * quarter + begin * quarter, size * quarter), :]

        for d in SIGNS:
            w = lambda piece=piece: piece(0, 0, 0)
            msg(("t1", h, d), w, w, lambda a1=a1, d=d: at_xy(a1, d), a1 + "+-"[d < 0], hb)
            w = lambda piece=piece, d=d: piece(-d, 0, d)
            msg(("t1q", h, d), w, w, lambda a1=a1, d=d: at_xy(a1, d), a1 + "+-"[d < 0], qb)
            for o in (0, -1, 1, 2):
                w = lambda piece=piece, o=o: piece(o, 0, 0)
                msg(("t2", h, o, d), w, w, lambda a2=a2, d=d: at_xy(a2, d), a2 + "+-"[d < 0], hb)
                w = lambda piece=piece, o=o, d=d: piece(o, -d, d)
                msg(("t2q", h, o, d), w, w, lambda a2=a2, d=d: at_xy(a2, d), a2 + "+-"[d < 0], qb)
                token_msgs += [("t2", h, o, d), ("t2q", h, o, d)]
            token_msgs += [("t1", h, d), ("t1q", h, d)]
        for o in (0, -1, 1, 2):
            for u in (0, -1, 1, 2):
                w = lambda piece=piece, o=o, u=u: piece(o, u, 0)
                msg(("td", h, o, u), w, w, lambda: at_quad(1), "d", hb)
                token_msgs.append(("td", h, o, u))
        have = {0: [], -1: [("t1", h, 1)], 1: [("t1", h, -1)], 2: [("t1q", h, 1), ("t1q", h, -1)]}
        task(("tok1", h), deps=[], sends=[("t1", h, 1), ("t1", h, -1)], prio=0)
        for d in SIGNS:
            task(("tok1q", h, d), deps=[("t1", h, d)], sends=[("t1q", h, d)], prio=1)
        for o in (0, -1, 1, 2):
            task(("tok2", h, o), deps=have[o] + [("tok1", h)], sends=[("t2", h, o, 1), ("t2", h, o, -1)], prio=2)
            for d in SIGNS:
                task(("tok2q", h, o, d), deps=[("t2", h, o, d)], sends=[("t2q", h, o, d)], prio=2)
            there = {0: have[o], -1: [("t2", h, o, 1)], 1: [("t2", h, o, -1)], 2: [("t2q", h, o, 1), ("t2q", h, o, -1)]}
            for u in (0, -1, 1, 2):
                task(("tokd", h, o, u), deps=there[u], sends=[("td", h, o, u)], prio=3)
    task("tok_first", deps=[("tok1", 0), ("tok1", 1)], prio=0)
    task("tok_all", deps=token_msgs, prio=4)

    def first_matmul(e, far):
        zs = wrap(z - e, nz)
        hf = 1 - xh if far else xh

        def tile(rr, carry):
            lhs = tok[zs, rr, :, pl.ds(pl.multiple_of(hf * 256, 256), 256)]
            rhs = wb[zs, pl.ds(hf * 2, 2)].reshape(256, 384)
            acc[rr] += jnp.dot(lhs, rhs, preferred_element_type=F32)
            return carry

        lax.fori_loop(0, 4, tile, 0)

    mm = []
    for far in (False, True):
        for e in range(-half_z + 1, half_z + 1):
            pair = (2, 3) if far else (0, 1)
            if e == 0:
                deps = [("wq", m) for m in pair if m]
            elif e == half_z:
                d = -1 if far else 1
                deps = [("w", m, d, half_z) for m in pair]
            else:
                deps = [("w", m, 1 if e > 0 else -1, abs(e)) for m in pair]
            mm.append(task(("mm", e, far), deps=["tok_all"] + deps, run=lambda e=e, far=far: first_matmul(e, far), cost=0.55, prio=6))

    def build_toeplitz():
        for q in range(4):
            lfs[q] = lf[q * ngroups : (q + 1) * ngroups, :].astype(F32)
        for j in range(3):
            sfs[3 * j : 3 * j + 3, :] = sf[j, :, lanes(r)]

        def one(g, carry):
            row = lfs[r, pl.ds(g, 1), :]
            line = jnp.concatenate([row, jnp.zeros_like(row)], axis=1)
            skew = pltpu.roll(jnp.broadcast_to(line, (256, 256)), 0, 1, stride=1, stride_axis=0).astype(BF16)
            toe[g, 0:128, :] = skew[128:256, 0:128]
            toe[g, 128:256, :] = skew[0:128, 0:128]
            voe[g] = skew[0:128, :]
            return carry

        lax.fori_loop(0, ngroups, one, 0)
        sfs[...] = sfs[...].T

    task("toe", run=build_toeplitz, cost=3.0, prio=8)

    def turn_gout():
        flat = go[...].reshape(ntok, 128).T
        gox[:, :, 0:ntok] = flat.reshape(ngroups, members, ntok)

    msg("goh", lambda: gox.at[:, :, pl.ds(0, 256)], lambda: gox.at[:, :, pl.ds(ntok, 256)], lambda: at_z(-1), "z-", 128 * 512)
    task("got", deps=[("goq", 1), ("goq", 2), ("goq", 3)], run=turn_gout, sends=["goh"], cost=0.6, prio=7)

    def turn_mixed():
        for i in range(3):
            flat = acc[:, :, i * 128 : (i + 1) * 128].reshape(ntok, 128).astype(BF16).T
            mx[i, :, :, 256 : 256 + ntok] = flat.reshape(ngroups, members, ntok)

    msg(("mh", 1), lambda: mx.at[:, :, :, pl.ds(ntok, 256)], lambda: mx.at[:, :, :, pl.ds(0, 256)], lambda: at_z(1), "z+", 384 * 512)
    msg(("mh", -1), lambda: mx.at[:, :, :, pl.ds(256, 256)], lambda: mx.at[:, :, :, pl.ds(256 + ntok, 256)], lambda: at_z(-1), "z-", 384 * 512)
    task("mxt", deps=mm, run=turn_mixed, sends=[("mh", 1), ("mh", -1)], cost=1.5, prio=0)

    span = ntok + 128

    def local_operator():
        lane = lax.broadcasted_iota(jnp.int32, (members, 128), 1)
        flip = (
            lax.broadcasted_iota(jnp.int32, (128, 128), 0) + lax.broadcasted_iota(jnp.int32, (128, 128), 1) == 127
        ).astype(F32).astype(BF16)
        width = ntok + 512
        position = lax.broadcasted_iota(jnp.int32, (members, width), 1)
        low = jnp.where(z == 0, 256, 0)
        high = jnp.where(z == nz - 1, 256 + ntok, width)
        inside = (position >= low) & (position < high)

        def group(g, carry):
            taps = sfs[pl.ds(pl.multiple_of(g * members, members), members), :]

            def tap(j, i):
                return taps[:, 3 * j + i : 3 * j + i + 1]

            lag, feats = [], []
            for i in range(3):
                base = jnp.where(inside, mx[i, g].astype(F32), 0.0)
                lag.append([base, pltpu.roll(base, 1, 1), pltpu.roll(base, 2, 1)])
                feats.append(tap(0, i) * lag[i][0] + tap(1, i) * lag[i][1] + tap(2, i) * lag[i][2])
            product = (feats[1] * feats[2]).astype(BF16)
            windows = jnp.concatenate([product[:, 128 * (b + 1) : 128 * (b + 3)] for b in range(nblocks + 1)], axis=0)
            out = jnp.dot(windows, toe[g], preferred_element_type=F32)
            conv = jnp.concatenate([out[members * b : members * (b + 1)] for b in range(nblocks + 1)], axis=1)
            up = jnp.where(inside[:, 256:], gox[g].astype(F32), 0.0)
            query = feats[0][:, 256:]
            gconv = (up * query).astype(BF16)
            ahead = jnp.concatenate([gconv[:, 128 * b : 128 * (b + 2)] for b in range(nblocks + 1)], axis=0)
            back = lax.dot_general(ahead, voe[g], (((1,), (1,)), ((), ())), preferred_element_type=F32)
            gproduct = jnp.concatenate([back[members * b : members * (b + 1)] for b in range(nblocks + 1)], axis=1)
            mxo[g] = (query[:, :ntok] * conv[:, :ntok]).astype(BF16)
            gfeats = [
                up[:, :span] * conv,
                gproduct * feats[2][:, 256 : 256 + span],
                gproduct * feats[1][:, 256 : 256 + span],
            ]
            sums = jnp.zeros((members, 128), F32)
            for i in range(3):
                grad = tap(0, i) * gfeats[i] + tap(1, i) * pltpu.roll(gfeats[i], span - 1, 1) + tap(2, i) * pltpu.roll(gfeats[i], span - 2, 1)
                gmt[i, g] = grad[:, :ntok].astype(BF16)
                for j in range(3):
                    both = gfeats[i][:, :ntok] * lag[i][j][:, 256 : 256 + ntok]
                    part = both[:, 0:128]
                    for b in range(1, nblocks):
                        part = part + both[:, 128 * b : 128 * (b + 1)]
                    sums = jnp.where(lane == 3 * j + i, jnp.sum(part, axis=1, keepdims=True), sums)
            gsb[pl.ds(pl.multiple_of(g * members, members), members), :] = sums
            held = jnp.concatenate([gconv[:, 128 * b : 128 * (b + 1)] for b in range(nblocks)], axis=0)
            flipped = jnp.dot(held, flip, preferred_element_type=F32).astype(BF16)
            pairs = lax.dot_general(flipped, windows[: members * nblocks], (((0,), (0,)), ((), ())), preferred_element_type=F32)
            skew = pltpu.roll(pairs, 0, 1, stride=1, stride_axis=0)
            glb[pl.ds(g, 1), :] = jnp.sum(skew, axis=0, keepdims=True)[:, 128:]
            return carry

        lax.fori_loop(0, ngroups, group, 0)
        unflipped = jnp.dot(glb[...].astype(BF16), flip, preferred_element_type=F32)
        smv[0:8, :] = unflipped
        smv[8:24, :] = gsb[...].T[0:16, :]

    task("local", deps=[("mh", 1), ("mh", -1), "goh", "toe", "got", "mxt"], run=local_operator, cost=9.0, prio=0)

    for m in (1, 2, 3):
        link, hops = ("d", 1) if m == 1 else ("x-", 2)
        msg(
            ("mq", m), lambda m=m: mxt.at[pl.ds(pl.multiple_of(mate(m) * rows, rows), rows), :], lambda: mr.at[r],
            lambda m=m: at_quad(m), link, rows * 256, hops,
        )
        msg(("sq", m), lambda: smt, lambda m=m: sqr.at[m - 1], lambda m=m: at_quad(m), link, 24 * 512, hops)

    def turn_output():
        for g in range(ngroups):
            mxt[:, g * members : (g + 1) * members] = mxo[g].T

    task("mixed_send", deps=["local"], run=turn_output, sends=[("mq", m) for m in (1, 2, 3)], cost=0.7, prio=3.35)
    offsets = [e for e in range(-half_z + 1, half_z + 1) if e]
    for n, e in enumerate(offsets):
        msg(("sm", e), lambda: smv, lambda n=n: smr.at[n], lambda e=e: at_z(e), "z+" if e > 0 else "z-", 24 * 512, abs(e))
    task("small_send", deps=["local"], sends=[("sm", e) for e in offsets], prio=3.36)

    def small_total():
        total = smv[...]
        for n in range(len(offsets)):
            total = total + smr[n]
        smt[...] = total * scale

    task("small_sum", deps=[("sm", e) for e in offsets] + ["small_send"], run=small_total, sends=[("sq", m) for m in (1, 2, 3)], cost=0.1, prio=7)

    def small_out():
        for m in range(4):
            part = smt[...] if m == 0 else sqr[m - 1]
            q = mate(m)
            gl_out[pl.ds(pl.multiple_of(q * 8, 8), 8), :] = part[0:8]
            for j in range(3):
                gs_out[j, :, lanes(q)] = part[8 + 3 * j : 11 + 3 * j]

    task("small_out", deps=[("sq", m) for m in (1, 2, 3)] + ["small_sum"], run=small_out, cost=0.1, prio=9)

    def mixed_final():
        mixed_out[:, lanes(r)] = mxt[pl.ds(pl.multiple_of(r * rows, rows), rows), :]
        for m in (1, 2, 3):
            mixed_out[:, lanes(mate(m))] = mr[mate(m)]

    task("mixed_out", deps=[("mq", m) for m in (1, 2, 3)] + ["mixed_send"], run=mixed_final, cost=0.1, prio=9)

    def weight_partial(e):
        zc = wrap(z + e, nz)
        lhs = gmt[...].reshape(384, ntok)

        def tile(n, carry):
            rhs = tok[zc, :, :, pl.ds(pl.multiple_of(n * 256, 256), 256)].reshape(ntok, 256)
            out = jnp.dot(lhs, rhs, preferred_element_type=F32)
            gp[e % nz, 2 * n] = out[:, 0:128]
            gp[e % nz, 2 * n + 1] = out[:, 128:256]
            return carry

        lax.fori_loop(0, 2, tile, 0)

    chunks = [half_z]
    for e in range(half_z - 1, 0, -1):
        chunks += [e, -e]
    chunks.append(0)
    for n, e in enumerate(chunks):
        task(("gw", e % nz), deps=["local"], run=lambda e=e: weight_partial(e), cost=1.0, prio=3 + 0.1 * n)
    slot = {}
    for m in range(4):
        for d in SIGNS:
            top = reach(m, d, False) if m < 2 else reach(m, d, False)
            for h in range(top, 0, -1):
                slot[m, d, h] = len(slot)
    for m in (2, 3, 0, 1):
        for d in SIGNS:
            top = reach(m, d, False)
            for h in range(top, 0, -1):
                s = slot[m, d, h]
                name = msg(("wr", m, d, h), lambda s=s: ws.at[s], lambda s=s: wr.at[s], lambda d=d: at_z(d), "z+" if d > 0 else "z-", wbytes)
                deps = [("gw", (d * h) % nz)]
                if h < top:
                    deps.append(("wr", m, d, h + 1))

                def add(m=m, d=d, h=h, s=s, top=top):
                    value = gp[(d * h) % nz, mate(m)]
                    if h < top:
                        value = value + wr[slot[m, d, h + 1]].astype(F32)
                    ws[s] = value.astype(BF16)

                task(("send", "wr", m, d, h), deps=deps, run=add, sends=[name], cost=0.12, prio=0 if m >= 2 else 1)

    def weight_total(m):
        return (gp[0, mate(m)] + wr[slot[m, 1, 1]].astype(F32) + wr[slot[m, -1, 1]].astype(F32)) * scale

    def weight_store(m, value):
        for i in range(3):
            gw_out[i, :, lanes(mate(m))] = value[i * 128 : (i + 1) * 128, :].T

    for m in range(4):
        deps = [("gw", 0), ("wr", m, 1, 1), ("wr", m, -1, 1)]
        if m == 0:
            task("wtot0", deps=deps, run=lambda: weight_store(0, weight_total(0)), cost=0.5, prio=8)
            continue
        link, hops = ("d", 1) if m == 1 else ("x-" if m == 2 else "x+", 2)
        msg(("wf", m), lambda m=m: fs.at[m - 1], lambda m=m: fr.at[m - 1], lambda m=m: at_quad(m), link, wbytes, hops)

        def finish(m=m):
            fs[m - 1] = weight_total(m).astype(BF16)

        task(("wtot", m), deps=deps, run=finish, sends=[("wf", m)], cost=0.2, prio=1)
        task(("wout", m), deps=[("wf", m)], run=lambda m=m: weight_store(m, fr[m - 1].astype(F32)), cost=0.5, prio=8)

    def feature_block(dy, dx):
        return wrap(y + dy, 4) * 2 + wrap(xl + dx, 2)

    def token_partial(dy, dx):
        k = feature_block(dy, dx)
        rhs = wb[k].reshape(512, 384)

        def tile(rr, carry):
            lhs = gm[pl.ds(pl.multiple_of(rr * rows, rows), rows), :]
            pp[k, rr] = lax.dot_general(lhs, rhs, (((1,), (1,)), ((), ())), preferred_element_type=F32).astype(BF16)
            return carry

        lax.fori_loop(0, 4, tile, 0)

    def pair_sum(dy, dx):
        k = feature_block(dy, dx)
        for ph in range(2):
            pp[k, ph * 2 + c] = (pp[k, ph * 2 + c].astype(F32) + pr[k, ph].astype(F32)).astype(BF16)

    def turn_grad():
        for i in range(3):
            gm[:, i * 128 : (i + 1) * 128] = gmt[i].reshape(128, ntok).T

    task("turn_grad", deps=["local"], run=turn_grad, cost=1.0, prio=3.15)
    for n, dy in enumerate((2, 1, -1, 0)):
        for dx in (0, 1):
            both = [
                msg(
                    ("pd", dy, dx, ph), lambda dy=dy, dx=dx, ph=ph: pp.at[feature_block(dy, dx), ph * 2 + (1 - c)],
                    lambda dy=dy, dx=dx, ph=ph: pr.at[feature_block(dy, dx), ph], lambda: at_quad(1), "d", rows * cols * 2,
                )
                for ph in range(2)
            ]
            task(("pk", dy, dx), deps=["turn_grad"], run=lambda dy=dy, dx=dx: token_partial(dy, dx), sends=both, cost=1.1, prio=3.21 + 0.12 * n + 0.06 * dx)
            task(("pa", dy, dx), deps=both + [("pk", dy, dx)], run=lambda dy=dy, dx=dx: pair_sum(dy, dx), cost=0.25, prio=2.5)

    def part_rows(h, part):
        begin, size = {0: (0, 2), 1: (0, 1), -1: (1, 1)}[part]
        return pl.ds(h * 2 * quarter + begin * quarter, size * quarter)

    def own_rows(part):
        return slice(0, quarter) if part > 0 else slice(quarter, 2 * quarter)

    for h in (0, 1):
        a1, a2 = ("y", "x") if h == 0 else ("x", "y")

        def needs(o1, o2, h=h):
            dy, dx = (o1, o2) if h == 0 else (o2, o1)
            dy = {0: 0, 1: 1, -1: -1, 2: 2}[dy]
            return ("pa", dy, dx % 2)

        def held(o1, o2, part, h=h, a1=a1):
            k, ph = place(a1, o1, o2)
            return pp.at[k, ph * 2 + c, part_rows(h, part), :]

        for o in (2, 1, -1, 0):
            oi = o % 4
            for d in SIGNS:
                di = 0 if d > 0 else 1
                link1 = a1 + "+-"[d < 0]
                msg(("s1q", h, o, d), lambda held=held, o=o, d=d: held(2, o, d), lambda h=h, oi=oi, di=di: q1.at[h, oi, di], lambda a1=a1, d=d: at_xy(a1, d), link1, qb)
                msg(("s1h", h, o, d), lambda h=h, oi=oi, di=di: h1s.at[h, oi, di], lambda h=h, oi=oi, di=di: h1.at[h, oi, di], lambda a1=a1, d=d: at_xy(a1, d), link1, hb)
                task(("s1q", h, o, d, "go"), deps=[needs(2, o)], sends=[("s1q", h, o, d)], prio=1)

                def forward(h=h, o=o, oi=oi, d=d, di=di, held=held):
                    own = held(d, o, 0)[...]
                    mine, rest = own_rows(d), own_rows(-d)
                    h1s[h, oi, di, mine, :] = (own[mine].astype(F32) + q1[h, oi, di].astype(F32)).astype(BF16)
                    h1s[h, oi, di, rest, :] = own[rest]

                task(("s1h", h, o, d, "go"), deps=[("s1q", h, o, d), needs(d, o)], run=forward, sends=[("s1h", h, o, d)], cost=0.08, prio=2)

            def settle(h=h, o=o, oi=oi, held=held):
                total = held(0, o, 0)[...].astype(F32) + h1[h, oi, 0].astype(F32) + h1[h, oi, 1].astype(F32)
                s1[h, oi] = total.astype(BF16)

            sends = []
            if o == 2:
                for d in SIGNS:
                    di = 0 if d > 0 else 1
                    part = slice(0, quarter) if d > 0 else slice(quarter, 2 * quarter)
                    begin = 0 if d > 0 else quarter
                    sends.append(
                        msg(("s2q", h, d), lambda h=h, begin=begin: s1.at[h, 2, pl.ds(begin, quarter), :], lambda h=h, di=di: q2.at[h, di], lambda a2=a2, d=d: at_xy(a2, d), a2 + "+-"[d < 0], qb)
                    )
            task(("s1", h, o), deps=[("s1h", h, o, 1), ("s1h", h, o, -1), needs(0, o)], run=settle, sends=sends, cost=0.08, prio=2)
        for d in SIGNS:
            di = 0 if d > 0 else 1
            msg(("s2h", h, d), lambda h=h, di=di: h2s.at[h, di], lambda h=h, di=di: h2.at[h, di], lambda a2=a2, d=d: at_xy(a2, d), a2 + "+-"[d < 0], hb)

            def second(h=h, d=d, di=di):
                own = s1[h, d % 4]
                mine, rest = own_rows(d), own_rows(-d)
                h2s[h, di, mine, :] = (own[mine].astype(F32) + q2[h, di].astype(F32)).astype(BF16)
                h2s[h, di, rest, :] = own[rest]

            task(("s2h", h, d, "go"), deps=[("s2q", h, d), ("s1", h, d)], run=second, sends=[("s2h", h, d)], cost=0.08, prio=2)

        def last(h=h):
            total = s1[h, 0].astype(F32) + h2[h, 0].astype(F32) + h2[h, 1].astype(F32)
            gin_out[h * 2 * quarter : (h + 1) * 2 * quarter, :] = total.astype(BF16)

        task(("gin", h), deps=[("s2h", h, 1), ("s2h", h, -1), ("s1", h, 0)], run=last, cost=0.1, prio=8)

    for q in range(4):
        for i in range(3):
            wst[q, :, i * 128 : (i + 1) * 128] = w3[i, :, q * 128 : (q + 1) * 128]
    for i in range(3):
        wb[z, r, :, i * 128 : (i + 1) * 128] = w3[i, :, lanes(r)]
    k_me, _ = place("x", 0, 0)
    tok[k_me, r] = tokens[...]
    go[r] = gout[:, lanes(r)]
    acc[...] = jnp.zeros_like(acc)
    sfs[...] = jnp.zeros_like(sfs)
    barrier = pltpu.get_barrier_semaphore()
    peers = [at_z(e) for e in offsets] + [at_quad(m) for m in (1, 2, 3)] + [at_xy(a, d) for a in ("x", "y") for d in SIGNS]
    for peer in peers:
        pl.semaphore_signal(barrier, inc=1, device_id=peer, device_id_type=MESH)
    pl.semaphore_wait(barrier, len(peers))

    order, _ = planned_order(tasks, msgs)
    waited = set()
    for step in order:
        for dep in step["deps"]:
            if dep in msgs and dep not in waited:
                copy_of(dep).wait_recv()
                waited.add(dep)
        if step["run"] is not None:
            step["run"]()
        for name in step["sends"]:
            copy_of(name).start()
    for name in msgs:
        copy_of(name).wait_send()


def scratch(nz, rows, cols, n_messages):
    ntok = 4 * rows
    quarter = rows // 4
    v = pltpu.VMEM
    return [
        v((nz, 4, rows, cols), BF16),
        v((4, 128, 384), BF16),
        v((nz, 4, 128, 384), BF16),
        v((4, rows, 128), BF16),
        v((4, rows, 384), F32),
        v((3, 8, 16, ntok + 512), BF16),
        v((8, 16, ntok + 256), BF16),
        v((8, 256, 128), BF16),
        v((8, 128, 256), BF16),
        v((4, 8, 128), F32),
        v((128, 128), F32),
        v((8, 16, ntok), BF16),
        v((ntok, 128), BF16),
        v((4, rows, 128), BF16),
        v((3, 8, 16, ntok), BF16),
        v((ntok, 384), BF16),
        v((8, 128), F32),
        v((128, 128), F32),
        v((24, 128), F32),
        v((nz - 1, 24, 128), F32),
        v((24, 128), F32),
        v((3, 24, 128), F32),
        v((nz, 4, 384, 128), F32),
        v((4 * (nz - 1), 384, 128), BF16),
        v((4 * (nz - 1), 384, 128), BF16),
        v((3, 384, 128), BF16),
        v((3, 384, 128), BF16),
        v((8, 4, rows, cols), BF16),
        v((8, 2, rows, cols), BF16),
        v((2, 4, 2, quarter, cols), BF16),
        v((2, 4, 2, 2 * quarter, cols), BF16),
        v((2, 4, 2, 2 * quarter, cols), BF16),
        v((2, 4, 2 * quarter, cols), BF16),
        v((2, 2, quarter, cols), BF16),
        v((2, 2, 2 * quarter, cols), BF16),
        v((2, 2, 2 * quarter, cols), BF16),
        pltpu.SemaphoreType.DMA((n_messages,)),
        pltpu.SemaphoreType.DMA((n_messages,)),
    ]


def per_device(tokens, in_weight, short_filter, long_filter, grad_out):
    rows, cols = tokens.shape
    nz = lax.axis_size("dp") // 4
    scale = float(rows * 4 * nz) ** (-0.5)
    vmem = pl.BlockSpec(memory_space=pltpu.VMEM)

    def body(*refs):
        block_kernel(*refs, nz=nz, scale=scale)

    mixed, grad_in, grad_w, grad_long, grad_short = pl.pallas_call(
        body,
        out_shape=(
            jax.ShapeDtypeStruct((rows, cols), BF16),
            jax.ShapeDtypeStruct((rows, cols), BF16),
            jax.ShapeDtypeStruct((3, 128, cols), F32),
            jax.ShapeDtypeStruct((32, 128), F32),
            jax.ShapeDtypeStruct((3, 3, cols), F32),
        ),
        in_specs=[vmem] * 5,
        out_specs=(vmem,) * 5,
        scratch_shapes=scratch(nz, rows, cols, 256),
        compiler_params=pltpu.CompilerParams(
            collective_id=0, has_side_effects=True, vmem_limit_bytes=62 * 1024 * 1024
        ),
        name="hyena_block",
    )(tokens, in_weight.transpose(1, 0, 2), short_filter, long_filter, grad_out)
    return mixed, grad_in, grad_w.transpose(1, 0, 2), grad_long, grad_short


def solution(mesh):
    placed = (
        P("dp", ("row", "col")),
        P("dp", None, ("row", "col")),
        P(None, None, ("row", "col")),
        P(("row", "col"), None),
        P("dp", ("row", "col")),
    )
    return jax.shard_map(
        per_device,
        mesh=mesh,
        in_specs=placed,
        out_specs=(
            P("dp", ("row", "col")),
            P("dp", ("row", "col")),
            P("dp", None, ("row", "col")),
            P(("row", "col"), None),
            P(None, None, ("row", "col")),
        ),
        check_vma=False,
    )
```

```python
import jax
import jax.numpy as jnp
from jax import lax
from jax.experimental import pallas as pl
from jax.experimental.pallas import tpu as pltpu
from jax.sharding import PartitionSpec as P

MESH = pl.DeviceIdType.MESH
F32, BF16 = jnp.float32, jnp.bfloat16
SIGNS = (1, -1)
UNROLL = 1
LINK_RATE = {"z": 46.0e3, "x": 46.0e3, "y": 46.0e3, "d": 200.0e3}
LINK_LATENCY = {"z": 1.6, "x": 1.6, "y": 1.6, "d": 1.0}


def planned_order(tasks, msgs):
    arrival, done, link_free = {}, {}, {}
    left, order, now = list(tasks), [], 0.0
    while left:
        best = None
        for at, task in enumerate(left):
            ready = 0.0
            for dep in task["deps"]:
                when = arrival.get(dep, done.get(dep))
                if when is None:
                    ready = None
                    break
                ready = max(ready, when)
            if ready is None:
                continue
            key = (max(ready, now), task["prio"], ready, at)
            if best is None or key < best[0]:
                best = (key, at)
        task = left.pop(best[1])
        now = best[0][0] + task["cost"]
        done[task["name"]] = now
        order.append(task)
        for name in task["sends"]:
            link, nbytes, hops = msgs[name]["link"], msgs[name]["bytes"], msgs[name]["hops"]
            begin = max(now, link_free.get(link, 0.0))
            link_free[link] = begin + nbytes * hops / LINK_RATE[link[0]]
            arrival[name] = link_free[link] + LINK_LATENCY[link[0]] * hops
    return order, now


def block_kernel(
    tokens, w3, sf, lf, gout, mixed_out, gin_out, gw_out, gl_out, gs_out,
    tok, wst, wb, go, acc, before, after, edge, mx, gox, toe, voe, lfs, sfs, mxo, mxt, mr, gmt, gm,
    gcs, pds, gfs, glb, gsb, smv, smr, smt, sqr, gp, ws, wr, fs, fr, pp, pr, q1, h1s, h1, s1, q2, h2s, h2,
    ssem, rsem, *, nz, scale,
):
    dp, y, xl = lax.axis_index("dp"), lax.axis_index("row"), lax.axis_index("col")
    z, r = dp // 4, dp % 4
    xh, c = r // 2, r % 2
    x = xh * 2 + xl
    rows, cols = tokens.shape
    quarter = rows // 4
    ntok = 4 * rows
    ngroups, members = mx.shape[1], mx.shape[2]
    nblocks = ntok // 128
    half_z = nz // 2

    def wrap(value, n):
        return lax.rem(value + 2 * n, n)

    def mate(m):
        other_h = 1 - xh if m & 2 else xh
        other_c = 1 - c if m & 1 else c
        return other_h * 2 + other_c

    def at_z(e):
        return (wrap(z + e, nz) * 4 + r, y, xl)

    def at_quad(m):
        return (z * 4 + mate(m), y, xl)

    def at_xy(axis, d):
        if axis == "y":
            return (dp, wrap(y + d, 4), xl)
        there = wrap(x + d, 4)
        return (z * 4 + (there // 2) * 2 + c, y, there % 2)

    def place(axis, first, second):
        dx, dy = (first, second) if axis == "x" else (second, first)
        px, py = wrap(x + dx, 4), wrap(y + dy, 4)
        return py * 2 + px % 2, px // 2

    msgs, tasks = {}, []

    def msg(name, src, dst, dev, link, nbytes, hops=1):
        msgs[name] = dict(src=src, dst=dst, dev=dev, link=link, bytes=nbytes, hops=hops, index=len(msgs))
        return name

    def task(name, deps=(), run=None, sends=(), cost=0.02, prio=5):
        tasks.append(dict(name=name, deps=list(deps), run=run, sends=list(sends), cost=cost, prio=prio))
        return name

    def copy_of(name):
        m = msgs[name]
        i = m["index"]
        return pltpu.make_async_remote_copy(
            src_ref=m["src"](), dst_ref=m["dst"](), send_sem=ssem.at[i], recv_sem=rsem.at[i],
            device_id=m["dev"](), device_id_type=MESH,
        )

    def lanes(block):
        return pl.ds(pl.multiple_of(block * 128, 128), 128)

    wbytes = 128 * 384 * 2
    for m in (1, 2, 3):
        link, hops = ("d", 1) if m == 1 else ("x+", 2)
        msg(("wq", m), lambda m=m: wst.at[mate(m)], lambda: wb.at[z, r], lambda m=m: at_quad(m), link, wbytes, hops)
        msg(("goq", m), lambda m=m: gout.at[:, lanes(mate(m))], lambda: go.at[r], lambda m=m: at_quad(m), link, rows * 256, hops)
    task("quad_w", sends=[("wq", 1), ("wq", 2), ("wq", 3)], prio=0)
    task("quad_go", deps=["quad_w", "tok_first"], sends=[("goq", 1), ("goq", 2), ("goq", 3)], prio=1)

    def reach(m, d, gather):
        return half_z if (m < 2) == (d > 0) else half_z - 1

    for m in range(4):
        for d in SIGNS:
            for h in range(1, reach(m, d, True) + 1):
                where = lambda m=m, d=d, h=h: wb.at[wrap(z - d * (h - 1), nz), mate(m)]
                name = msg(("w", m, d, h), where, where, lambda d=d: at_z(d), "z+" if d > 0 else "z-", wbytes)
                if h > 1:
                    deps = [("w", m, d, h - 1)]
                else:
                    deps = [("wq", m)] if m else []
                task(("send", name), deps=deps, sends=[name], prio=0 if m < 2 else 1)

    hb, qb = 2 * quarter * cols * 2, quarter * cols * 2
    token_msgs = []
    for h in (0, 1):
        a1, a2 = ("x", "y") if h == 0 else ("y", "x")

        def piece(o, u, part, h=h, a1=a1):
            k, ph = place(a1, o, u)
            begin, size = {0: (0, 2), 1: (0, 1), -1: (1, 1)}[part]
            return tok.at[k, ph * 2 + c, pl.ds(h * 2 * quarter + begin * quarter, size * quarter), :]

        for d in SIGNS:
            w = lambda piece=piece: piece(0, 0, 0)
            msg(("t1", h, d), w, w, lambda a1=a1, d=d: at_xy(a1, d), a1 + "+-"[d < 0], hb)
            w = lambda piece=piece, d=d: piece(-d, 0, d)
            msg(("t1q", h, d), w, w, lambda a1=a1, d=d: at_xy(a1, d), a1 + "+-"[d < 0], qb)
            for o in (0, -1, 1, 2):
                w = lambda piece=piece, o=o: piece(o, 0, 0)
                msg(("t2", h, o, d), w, w, lambda a2=a2, d=d: at_xy(a2, d), a2 + "+-"[d < 0], hb)
                w = lambda piece=piece, o=o, d=d: piece(o, -d, d)
                msg(("t2q", h, o, d), w, w, lambda a2=a2, d=d: at_xy(a2, d), a2 + "+-"[d < 0], qb)
                token_msgs += [("t2", h, o, d), ("t2q", h, o, d)]
            token_msgs += [("t1", h, d), ("t1q", h, d)]
        for o in (0, -1, 1, 2):
            for u in (0, -1, 1, 2):
                w = lambda piece=piece, o=o, u=u: piece(o, u, 0)
                msg(("td", h, o, u), w, w, lambda: at_quad(1), "d", hb)
                token_msgs.append(("td", h, o, u))
        have = {0: [], -1: [("t1", h, 1)], 1: [("t1", h, -1)], 2: [("t1q", h, 1), ("t1q", h, -1)]}
        task(("tok1", h), deps=[], sends=[("t1", h, 1), ("t1", h, -1)], prio=0)
        for d in SIGNS:
            task(("tok1q", h, d), deps=[("t1", h, d)], sends=[("t1q", h, d)], prio=1)
        for o in (0, -1, 1, 2):
            task(("tok2", h, o), deps=have[o] + [("tok1", h)], sends=[("t2", h, o, 1), ("t2", h, o, -1)], prio=2)
            for d in SIGNS:
                task(("tok2q", h, o, d), deps=[("t2", h, o, d)], sends=[("t2q", h, o, d)], prio=2)
            there = {0: have[o], -1: [("t2", h, o, 1)], 1: [("t2", h, o, -1)], 2: [("t2q", h, o, 1), ("t2q", h, o, -1)]}
            for u in (0, -1, 1, 2):
                task(("tokd", h, o, u), deps=there[u], sends=[("td", h, o, u)], prio=3)
    task("tok_first", deps=[("tok1", 0), ("tok1", 1)], prio=0)
    task("tok_all", deps=token_msgs, prio=4)

    started = []

    def first_matmul(e, far):
        zs = wrap(z - e, nz)
        hf = 1 - xh if far else xh

        lhs = tok[zs, :, :, pl.ds(pl.multiple_of(hf * 256, 256), 256)].reshape(ntok, 256)
        rhs = wb[zs, pl.ds(hf * 2, 2)].reshape(256, 384)
        out = jnp.dot(lhs, rhs, preferred_element_type=F32)
        acc[...] = out + acc[...] if started else out
        started.append(e)

    mm = []
    for far in (False, True):
        for e in range(-half_z + 1, half_z + 1):
            pair = (2, 3) if far else (0, 1)
            if e == 0:
                deps = [("wq", m) for m in pair if m]
            elif e == half_z:
                d = -1 if far else 1
                deps = [("w", m, d, half_z) for m in pair]
            else:
                deps = [("w", m, 1 if e > 0 else -1, abs(e)) for m in pair]
            mm.append(task(("mm", e, far), deps=["tok_all"] + deps, run=lambda e=e, far=far: first_matmul(e, far), cost=0.45, prio=6))

    def build_toeplitz():
        for q in range(4):
            lfs[q] = lf[q * ngroups : (q + 1) * ngroups, :].astype(F32)
        for j in range(3):
            sfs[3 * j : 3 * j + 3, :] = sf[j, :, lanes(r)]

        def one(g, carry):
            row = lfs[r, pl.ds(g, 1), :]
            line = jnp.concatenate([row, jnp.zeros_like(row)], axis=1)
            skew = pltpu.roll(jnp.broadcast_to(line, (256, 256)), 0, 1, stride=1, stride_axis=0).astype(BF16)
            toe[g, 0:128, :] = skew[128:256, 0:128]
            toe[g, 128:256, :] = skew[0:128, 0:128]
            voe[g] = skew[0:128, :]
            return carry

        lax.fori_loop(0, ngroups, one, 0)
        sfs[...] = sfs[...].T

    task("toe", run=build_toeplitz, cost=3.0, prio=8)

    def turn_gout():
        flat = go[...].reshape(ntok, 128).T
        gox[:, :, 0:ntok] = flat.reshape(ngroups, members, ntok)

    msg("goh", lambda: gox.at[:, :, pl.ds(0, 256)], lambda: gox.at[:, :, pl.ds(ntok, 256)], lambda: at_z(-1), "z-", 128 * 512)
    task("got", deps=[("goq", 1), ("goq", 2), ("goq", 3)], run=turn_gout, sends=["goh"], cost=0.6, prio=7)

    def edge_rows():
        edge[0] = acc[0:144, :].astype(BF16)
        edge[1] = acc[ntok - 144 : ntok, :].astype(BF16)

    key, first = pl.ds(128, 256), pl.ds(0, 128)
    msg(("mh", 1, 1), lambda: edge.at[1, :, key], lambda: before.at[pl.ds(112, 144), key], lambda: at_z(1), "z+", 144 * 512)
    msg(("mh", 1, 0), lambda: edge.at[1, pl.ds(128, 16), first], lambda: before.at[pl.ds(240, 16), first], lambda: at_z(1), "z+", 16 * 256)
    msg(("mh", -1, 0), lambda: edge.at[0, :, first], lambda: after.at[pl.ds(0, 144), first], lambda: at_z(-1), "z-", 144 * 256)
    msg(("mh", -1, 1), lambda: edge.at[0, pl.ds(0, 16), key], lambda: after.at[pl.ds(0, 16), key], lambda: at_z(-1), "z-", 16 * 512)
    halos = [("mh", 1, 1), ("mh", 1, 0), ("mh", -1, 0), ("mh", -1, 1)]
    task("edge", deps=mm, run=edge_rows, sends=halos, cost=0.1, prio=0)

    def turn_mixed():
        for i in range(3):
            flat = acc[:, i * 128 : (i + 1) * 128].astype(BF16).T
            mx[i, :, :, 256 : 256 + ntok] = flat.reshape(ngroups, members, ntok)

    task("mxt", deps=["edge"], run=turn_mixed, cost=0.4, prio=0)

    def turn_halos():
        for i in range(3):
            for buf, off, dead in ((before, 0, z == 0), (after, 256 + ntok, z == nz - 1)):
                flat = buf[:, i * 128 : (i + 1) * 128].T
                mx[i, :, :, off : off + 256] = jnp.where(dead, jnp.zeros_like(flat), flat).reshape(ngroups, members, 256)
        ahead = gox[:, :, ntok : ntok + 256]
        gox[:, :, ntok : ntok + 256] = jnp.where(z == nz - 1, jnp.zeros_like(ahead), ahead)

    task("halo", deps=halos + ["goh", "mxt", "got"], run=turn_halos, cost=0.3, prio=0)

    span = ntok + 128

    def tap_of(g):
        taps = sfs[pl.ds(pl.multiple_of(g * members, members), members), :]
        return lambda j, i: taps[:, 3 * j + i : 3 * j + i + 1]

    def local_operator():
        def group(g, carry):
            tap = tap_of(g)
            feats = []
            for i in range(3):
                base = mx[i, g].astype(F32)
                feats.append(tap(0, i) * base + tap(1, i) * pltpu.roll(base, 1, 1) + tap(2, i) * pltpu.roll(base, 2, 1))
            product = (feats[1] * feats[2]).astype(BF16)
            pds[g] = product
            windows = jnp.concatenate([product[:, 128 * (b + 1) : 128 * (b + 3)] for b in range(nblocks + 1)], axis=0)
            out = jnp.dot(windows, toe[g], preferred_element_type=F32)
            conv = jnp.concatenate([out[members * b : members * (b + 1)] for b in range(nblocks + 1)], axis=1)
            up = gox[g].astype(F32)
            query = feats[0][:, 256:]
            gconv = (up * query).astype(BF16)
            gcs[g] = gconv[:, :ntok]
            ahead = jnp.concatenate([gconv[:, 128 * b : 128 * (b + 2)] for b in range(nblocks + 1)], axis=0)
            back = lax.dot_general(ahead, voe[g], (((1,), (1,)), ((), ())), preferred_element_type=F32)
            gproduct = jnp.concatenate([back[members * b : members * (b + 1)] for b in range(nblocks + 1)], axis=1)
            mxo[g] = (query[:, :ntok] * conv[:, :ntok]).astype(BF16)
            gfeats = [
                up[:, :span] * conv,
                gproduct * feats[2][:, 256 : 256 + span],
                gproduct * feats[1][:, 256 : 256 + span],
            ]
            for i in range(3):
                grad = tap(0, i) * gfeats[i] + tap(1, i) * pltpu.roll(gfeats[i], span - 1, 1) + tap(2, i) * pltpu.roll(gfeats[i], span - 2, 1)
                gmt[i, g] = grad[:, :ntok].astype(BF16)
                gfs[i, g] = gfeats[i][:, :ntok]
            return carry

        lax.fori_loop(0, ngroups, group, 0, unroll=UNROLL)

    task("local", deps=["halo", "toe"], run=local_operator, cost=6.0, prio=0)

    def filter_sums():
        lane = lax.broadcasted_iota(jnp.int32, (members, 128), 1)
        flip = (
            lax.broadcasted_iota(jnp.int32, (128, 128), 0) + lax.broadcasted_iota(jnp.int32, (128, 128), 1) == 127
        ).astype(F32).astype(BF16)

        def group(g, carry):
            sums = jnp.zeros((members, 128), F32)
            for i in range(3):
                base = mx[i, g, :, 128 : 256 + ntok].astype(F32)
                for j in range(3):
                    late = pltpu.roll(base, j, 1) if j else base
                    both = gfs[i, g] * late[:, 128:]
                    part = both[:, 0:128]
                    for b in range(1, nblocks):
                        part = part + both[:, 128 * b : 128 * (b + 1)]
                    sums = jnp.where(lane == 3 * j + i, jnp.sum(part, axis=1, keepdims=True), sums)
            gsb[pl.ds(pl.multiple_of(g * members, members), members), :] = sums
            windows = jnp.concatenate([pds[g, :, 128 * (b + 1) : 128 * (b + 3)] for b in range(nblocks)], axis=0)
            held = jnp.concatenate([gcs[g, :, 128 * b : 128 * (b + 1)] for b in range(nblocks)], axis=0)
            flipped = jnp.dot(held, flip, preferred_element_type=F32).astype(BF16)
            pairs = lax.dot_general(flipped, windows, (((0,), (0,)), ((), ())), preferred_element_type=F32)
            skew = pltpu.roll(pairs, 0, 1, stride=1, stride_axis=0)
            glb[pl.ds(g, 1), :] = jnp.sum(skew, axis=0, keepdims=True)[:, 128:]
            return carry

        lax.fori_loop(0, ngroups, group, 0)
        smv[0:8, :] = jnp.dot(glb[...].astype(BF16), flip, preferred_element_type=F32)
        smv[8:24, :] = gsb[...].T[0:16, :]

    for m in (1, 2, 3):
        link, hops = ("d", 1) if m == 1 else ("x-", 2)
        msg(
            ("mq", m), lambda m=m: mxt.at[pl.ds(pl.multiple_of(mate(m) * rows, rows), rows), :], lambda: mr.at[r],
            lambda m=m: at_quad(m), link, rows * 256, hops,
        )
        msg(("sq", m), lambda: smt, lambda m=m: sqr.at[m - 1], lambda m=m: at_quad(m), link, 24 * 512, hops)

    def turn_output():
        for g in range(ngroups):
            mxt[:, g * members : (g + 1) * members] = mxo[g].T

    task("mixed_send", deps=["local"], run=turn_output, sends=[("mq", m) for m in (1, 2, 3)], cost=0.3, prio=3.35)
    offsets = [e for e in range(-half_z + 1, half_z + 1) if e]
    for n, e in enumerate(offsets):
        msg(("sm", e), lambda: smv, lambda n=n: smr.at[n], lambda e=e: at_z(e), "z+" if e > 0 else "z-", 24 * 512, abs(e))
    task("small_send", deps=["local"], run=filter_sums, cost=4.0, sends=[("sm", e) for e in offsets], prio=3.9)

    def small_total():
        total = smv[...]
        for n in range(len(offsets)):
            total = total + smr[n]
        smt[...] = total * scale

    task("small_sum", deps=[("sm", e) for e in offsets] + ["small_send"], run=small_total, sends=[("sq", m) for m in (1, 2, 3)], cost=0.1, prio=7)

    def small_out():
        for m in range(4):
            part = smt[...] if m == 0 else sqr[m - 1]
            q = mate(m)
            gl_out[pl.ds(pl.multiple_of(q * 8, 8), 8), :] = part[0:8]
            for j in range(3):
                gs_out[j, :, lanes(q)] = part[8 + 3 * j : 11 + 3 * j]

    task("small_out", deps=[("sq", m) for m in (1, 2, 3)] + ["small_sum"], run=small_out, cost=0.1, prio=9)

    def mixed_final():
        mixed_out[:, lanes(r)] = mxt[pl.ds(pl.multiple_of(r * rows, rows), rows), :]
        for m in (1, 2, 3):
            mixed_out[:, lanes(mate(m))] = mr[mate(m)]

    task("mixed_out", deps=[("mq", m) for m in (1, 2, 3)] + ["mixed_send"], run=mixed_final, cost=0.1, prio=9)

    def weight_partial(e):
        zc = wrap(z + e, nz)
        out = jnp.dot(gmt[...].reshape(384, ntok), tok[zc].reshape(ntok, cols), preferred_element_type=F32)
        for n in range(4):
            gp[e % nz, n] = out[:, n * 128 : (n + 1) * 128]

    chunks = [half_z]
    for e in range(half_z - 1, 0, -1):
        chunks += [e, -e]
    chunks.append(0)
    for n, e in enumerate(chunks):
        task(("gw", e % nz), deps=["local"], run=lambda e=e: weight_partial(e), cost=0.6, prio=3 + 0.1 * n)
    slot = {}
    for m in range(4):
        for d in SIGNS:
            top = reach(m, d, False) if m < 2 else reach(m, d, False)
            for h in range(top, 0, -1):
                slot[m, d, h] = len(slot)
    for m in (2, 3, 0, 1):
        for d in SIGNS:
            top = reach(m, d, False)
            for h in range(top, 0, -1):
                s = slot[m, d, h]
                name = msg(("wr", m, d, h), lambda s=s: ws.at[s], lambda s=s: wr.at[s], lambda d=d: at_z(d), "z+" if d > 0 else "z-", wbytes)
                deps = [("gw", (d * h) % nz)]
                if h < top:
                    deps.append(("wr", m, d, h + 1))

                def add(m=m, d=d, h=h, s=s, top=top):
                    value = gp[(d * h) % nz, mate(m)]
                    if h < top:
                        value = value + wr[slot[m, d, h + 1]].astype(F32)
                    ws[s] = value.astype(BF16)

                task(("send", "wr", m, d, h), deps=deps, run=add, sends=[name], cost=0.12, prio=0 if m >= 2 else 1)

    def weight_total(m):
        return (gp[0, mate(m)] + wr[slot[m, 1, 1]].astype(F32) + wr[slot[m, -1, 1]].astype(F32)) * scale

    def weight_store(m, value):
        for i in range(3):
            gw_out[i, :, lanes(mate(m))] = value[i * 128 : (i + 1) * 128, :].T

    for m in range(4):
        deps = [("gw", 0), ("wr", m, 1, 1), ("wr", m, -1, 1)]
        if m == 0:
            task("wtot0", deps=deps, run=lambda: weight_store(0, weight_total(0)), cost=0.5, prio=8)
            continue
        link, hops = ("d", 1) if m == 1 else ("x-" if m == 2 else "x+", 2)
        msg(("wf", m), lambda m=m: fs.at[m - 1], lambda m=m: fr.at[m - 1], lambda m=m: at_quad(m), link, wbytes, hops)

        def finish(m=m):
            fs[m - 1] = weight_total(m).astype(BF16)

        task(("wtot", m), deps=deps, run=finish, sends=[("wf", m)], cost=0.2, prio=1)
        task(("wout", m), deps=[("wf", m)], run=lambda m=m: weight_store(m, fr[m - 1].astype(F32)), cost=0.5, prio=8)

    def feature_block(dy, dx):
        return wrap(y + dy, 4) * 2 + wrap(xl + dx, 2)

    def token_partial(dy, dx):
        k = feature_block(dy, dx)
        out = lax.dot_general(gm[...], wb[k].reshape(512, 384), (((1,), (1,)), ((), ())), preferred_element_type=F32)
        pp[k] = out.astype(BF16).reshape(4, rows, cols)

    def pair_sum(dy, dx):
        k = feature_block(dy, dx)
        for ph in range(2):
            pp[k, ph * 2 + c] = (pp[k, ph * 2 + c].astype(F32) + pr[k, ph].astype(F32)).astype(BF16)

    def turn_grad():
        for i in range(3):
            gm[:, i * 128 : (i + 1) * 128] = gmt[i].reshape(128, ntok).T

    task("turn_grad", deps=["local"], run=turn_grad, cost=0.3, prio=3.15)
    for n, dy in enumerate((2, 1, -1, 0)):
        for dx in (0, 1):
            both = [
                msg(
                    ("pd", dy, dx, ph), lambda dy=dy, dx=dx, ph=ph: pp.at[feature_block(dy, dx), ph * 2 + (1 - c)],
                    lambda dy=dy, dx=dx, ph=ph: pr.at[feature_block(dy, dx), ph], lambda: at_quad(1), "d", rows * cols * 2,
                )
                for ph in range(2)
            ]
            task(("pk", dy, dx), deps=["turn_grad"], run=lambda dy=dy, dx=dx: token_partial(dy, dx), sends=both, cost=0.75, prio=3.21 + 0.12 * n + 0.06 * dx)
            task(("pa", dy, dx), deps=both + [("pk", dy, dx)], run=lambda dy=dy, dx=dx: pair_sum(dy, dx), cost=0.25, prio=2.5)

    def part_rows(h, part):
        begin, size = {0: (0, 2), 1: (0, 1), -1: (1, 1)}[part]
        return pl.ds(h * 2 * quarter + begin * quarter, size * quarter)

    def own_rows(part):
        return slice(0, quarter) if part > 0 else slice(quarter, 2 * quarter)

    for h in (0, 1):
        a1, a2 = ("y", "x") if h == 0 else ("x", "y")

        def needs(o1, o2, h=h):
            dy, dx = (o1, o2) if h == 0 else (o2, o1)
            dy = {0: 0, 1: 1, -1: -1, 2: 2}[dy]
            return ("pa", dy, dx % 2)

        def held(o1, o2, part, h=h, a1=a1):
            k, ph = place(a1, o1, o2)
            return pp.at[k, ph * 2 + c, part_rows(h, part), :]

        for o in (2, 1, -1, 0):
            oi = o % 4
            for d in SIGNS:
                di = 0 if d > 0 else 1
                link1 = a1 + "+-"[d < 0]
                msg(("s1q", h, o, d), lambda held=held, o=o, d=d: held(2, o, d), lambda h=h, oi=oi, di=di: q1.at[h, oi, di], lambda a1=a1, d=d: at_xy(a1, d), link1, qb)
                msg(("s1h", h, o, d), lambda h=h, oi=oi, di=di: h1s.at[h, oi, di], lambda h=h, oi=oi, di=di: h1.at[h, oi, di], lambda a1=a1, d=d: at_xy(a1, d), link1, hb)
                task(("s1q", h, o, d, "go"), deps=[needs(2, o)], sends=[("s1q", h, o, d)], prio=1)

                def forward(h=h, o=o, oi=oi, d=d, di=di, held=held):
                    own = held(d, o, 0)[...]
                    mine, rest = own_rows(d), own_rows(-d)
                    h1s[h, oi, di, mine, :] = (own[mine].astype(F32) + q1[h, oi, di].astype(F32)).astype(BF16)
                    h1s[h, oi, di, rest, :] = own[rest]

                task(("s1h", h, o, d, "go"), deps=[("s1q", h, o, d), needs(d, o)], run=forward, sends=[("s1h", h, o, d)], cost=0.08, prio=2)

            def settle(h=h, o=o, oi=oi, held=held):
                total = held(0, o, 0)[...].astype(F32) + h1[h, oi, 0].astype(F32) + h1[h, oi, 1].astype(F32)
                s1[h, oi] = total.astype(BF16)

            sends = []
            if o == 2:
                for d in SIGNS:
                    di = 0 if d > 0 else 1
                    part = slice(0, quarter) if d > 0 else slice(quarter, 2 * quarter)
                    begin = 0 if d > 0 else quarter
                    sends.append(
                        msg(("s2q", h, d), lambda h=h, begin=begin: s1.at[h, 2, pl.ds(begin, quarter), :], lambda h=h, di=di: q2.at[h, di], lambda a2=a2, d=d: at_xy(a2, d), a2 + "+-"[d < 0], qb)
                    )
            task(("s1", h, o), deps=[("s1h", h, o, 1), ("s1h", h, o, -1), needs(0, o)], run=settle, sends=sends, cost=0.08, prio=2)
        for d in SIGNS:
            di = 0 if d > 0 else 1
            msg(("s2h", h, d), lambda h=h, di=di: h2s.at[h, di], lambda h=h, di=di: h2.at[h, di], lambda a2=a2, d=d: at_xy(a2, d), a2 + "+-"[d < 0], hb)

            def second(h=h, d=d, di=di):
                own = s1[h, d % 4]
                mine, rest = own_rows(d), own_rows(-d)
                h2s[h, di, mine, :] = (own[mine].astype(F32) + q2[h, di].astype(F32)).astype(BF16)
                h2s[h, di, rest, :] = own[rest]

            task(("s2h", h, d, "go"), deps=[("s2q", h, d), ("s1", h, d)], run=second, sends=[("s2h", h, d)], cost=0.08, prio=2)

        def last(h=h):
            total = s1[h, 0].astype(F32) + h2[h, 0].astype(F32) + h2[h, 1].astype(F32)
            gin_out[h * 2 * quarter : (h + 1) * 2 * quarter, :] = total.astype(BF16)

        task(("gin", h), deps=[("s2h", h, 1), ("s2h", h, -1), ("s1", h, 0)], run=last, cost=0.1, prio=8)

    for q in range(4):
        for i in range(3):
            wst[q, :, i * 128 : (i + 1) * 128] = w3[i, :, q * 128 : (q + 1) * 128]
    for i in range(3):
        wb[z, r, :, i * 128 : (i + 1) * 128] = w3[i, :, lanes(r)]
    k_me, _ = place("x", 0, 0)
    tok[k_me, r] = tokens[...]
    go[r] = gout[:, lanes(r)]
    before[...] = jnp.zeros_like(before)
    after[...] = jnp.zeros_like(after)
    sfs[...] = jnp.zeros_like(sfs)
    barrier = pltpu.get_barrier_semaphore()
    peers = [at_z(e) for e in SIGNS] + [at_quad(m) for m in (1, 2, 3)] + [at_xy(a, d) for a in ("x", "y") for d in SIGNS]
    for peer in peers:
        pl.semaphore_signal(barrier, inc=1, device_id=peer, device_id_type=MESH)
    pl.semaphore_wait(barrier, len(peers))

    order, _ = planned_order(tasks, msgs)
    waited = set()
    for step in order:
        for dep in step["deps"]:
            if dep in msgs and dep not in waited:
                copy_of(dep).wait_recv()
                waited.add(dep)
        if step["run"] is not None:
            step["run"]()
        for name in step["sends"]:
            copy_of(name).start()
    for name in msgs:
        copy_of(name).wait_send()


def scratch(nz, rows, cols, n_messages):
    ntok = 4 * rows
    quarter = rows // 4
    v = pltpu.VMEM
    return [
        v((nz, 4, rows, cols), BF16),
        v((4, 128, 384), BF16),
        v((nz, 4, 128, 384), BF16),
        v((4, rows, 128), BF16),
        v((ntok, 384), F32),
        v((256, 384), BF16),
        v((256, 384), BF16),
        v((2, 144, 384), BF16),
        v((3, 8, 16, ntok + 512), BF16),
        v((8, 16, ntok + 256), BF16),
        v((8, 256, 128), BF16),
        v((8, 128, 256), BF16),
        v((4, 8, 128), F32),
        v((128, 128), F32),
        v((8, 16, ntok), BF16),
        v((ntok, 128), BF16),
        v((4, rows, 128), BF16),
        v((3, 8, 16, ntok), BF16),
        v((ntok, 384), BF16),
        v((8, 16, ntok), BF16),
        v((8, 16, ntok + 512), BF16),
        v((3, 8, 16, ntok), F32),
        v((8, 128), F32),
        v((128, 128), F32),
        v((24, 128), F32),
        v((nz - 1, 24, 128), F32),
        v((24, 128), F32),
        v((3, 24, 128), F32),
        v((nz, 4, 384, 128), F32),
        v((4 * (nz - 1), 384, 128), BF16),
        v((4 * (nz - 1), 384, 128), BF16),
        v((3, 384, 128), BF16),
        v((3, 384, 128), BF16),
        v((8, 4, rows, cols), BF16),
        v((8, 2, rows, cols), BF16),
        v((2, 4, 2, quarter, cols), BF16),
        v((2, 4, 2, 2 * quarter, cols), BF16),
        v((2, 4, 2, 2 * quarter, cols), BF16),
        v((2, 4, 2 * quarter, cols), BF16),
        v((2, 2, quarter, cols), BF16),
        v((2, 2, 2 * quarter, cols), BF16),
        v((2, 2, 2 * quarter, cols), BF16),
        pltpu.SemaphoreType.DMA((n_messages,)),
        pltpu.SemaphoreType.DMA((n_messages,)),
    ]


def per_device(tokens, in_weight, short_filter, long_filter, grad_out):
    rows, cols = tokens.shape
    nz = lax.axis_size("dp") // 4
    scale = float(rows * 4 * nz) ** (-0.5)
    vmem = pl.BlockSpec(memory_space=pltpu.VMEM)

    def body(*refs):
        block_kernel(*refs, nz=nz, scale=scale)

    results = pl.pallas_call(
        body,
        out_shape=(
            jax.ShapeDtypeStruct((rows, cols), BF16),
            jax.ShapeDtypeStruct((rows, cols), BF16),
            jax.ShapeDtypeStruct((3, 128, cols), F32),
            jax.ShapeDtypeStruct((32, 128), F32),
            jax.ShapeDtypeStruct((3, 3, cols), F32),
        ),
        in_specs=[vmem] * 5,
        out_specs=(vmem,) * 5,
        scratch_shapes=scratch(nz, rows, cols, 256),
        compiler_params=pltpu.CompilerParams(
            collective_id=0, has_side_effects=True, vmem_limit_bytes=62 * 1024 * 1024
        ),
        name="hyena_block",
    )(tokens, in_weight.transpose(1, 0, 2), short_filter, long_filter, grad_out)

    def hand_over(*refs):
        for source, target in zip(refs[:5], refs[5:]):
            target[...] = source[...]

    mixed, grad_in, grad_w, grad_long, grad_short = pl.pallas_call(
        hand_over,
        out_shape=tuple(jax.ShapeDtypeStruct(a.shape, a.dtype) for a in results),
        in_specs=[vmem] * 5,
        out_specs=(vmem,) * 5,
        name="hand_over",
    )(*results)
    return mixed, grad_in, grad_w.transpose(1, 0, 2), grad_long, grad_short


def solution(mesh):
    placed = (
        P("dp", ("row", "col")),
        P("dp", None, ("row", "col")),
        P(None, None, ("row", "col")),
        P(("row", "col"), None),
        P("dp", ("row", "col")),
    )
    return jax.shard_map(
        per_device,
        mesh=mesh,
        in_specs=placed,
        out_specs=(
            P("dp", ("row", "col")),
            P("dp", ("row", "col")),
            P("dp", None, ("row", "col")),
            P(("row", "col"), None),
            P(None, None, ("row", "col")),
        ),
        check_vma=False,
    )
```

```python
import jax
import jax.numpy as jnp
from jax import lax
from jax.experimental import pallas as pl
from jax.experimental.pallas import tpu as pltpu
from jax.sharding import PartitionSpec as P

MESH = pl.DeviceIdType.MESH
F32, BF16 = jnp.float32, jnp.bfloat16
SIGNS = (1, -1)
UNROLL = 1
LINK_RATE = {"z": 46.0e3, "x": 46.0e3, "y": 46.0e3, "d": 600.0e3}
LINK_LATENCY = {"z": 1.6, "x": 1.6, "y": 1.6, "d": 1.0}


def planned_order(tasks, msgs):
    arrival, done, link_free = {}, {}, {}
    left, order, now = list(tasks), [], 0.0
    while left:
        best = None
        for at, task in enumerate(left):
            ready = 0.0
            for dep in task["deps"]:
                when = arrival.get(dep, done.get(dep))
                if when is None:
                    ready = None
                    break
                ready = max(ready, when)
            if ready is None:
                continue
            key = (max(ready, now), task["prio"], ready, at)
            if best is None or key < best[0]:
                best = (key, at)
        task = left.pop(best[1])
        now = best[0][0] + task["cost"]
        done[task["name"]] = now
        order.append(task)
        for name in task["sends"]:
            link, nbytes, hops = msgs[name]["link"], msgs[name]["bytes"], msgs[name]["hops"]
            arrival[name] = 0.0
            for one in ("x+", "x-") if link == "x2" else (link,):
                load = nbytes * (1 if link == "x2" else hops)
                begin = max(now, link_free.get(one, 0.0))
                link_free[one] = begin + load / LINK_RATE[one[0]]
                arrival[name] = max(arrival[name], link_free[one] + LINK_LATENCY[one[0]] * hops)
    return order, now


def block_kernel(
    tokens_hbm, w3_hbm, sf_hbm, lf_hbm, gout_hbm, mixed_out, gin_out, gw_out, gl_out, gs_out,
    w3, sf, lf, gout, tok, wst, wb, go, acc, before, after, edge, mx, gox, toe, voe, lfs, sfs, mxo, mxt, mr, gmt, gm,
    gcs, pds, gfs, glb, gsb, own_sums, smv, smr, smt, sqr, gp, ws, wr, fs, fr, pp, pr, q1, h1s, h1, s1, q2, h2s, h2,
    ssem, rsem, insem, *, nz, scale,
):
    dp, y, xl = lax.axis_index("dp"), lax.axis_index("row"), lax.axis_index("col")
    z, r = dp // 4, dp % 4
    xh, c = r // 2, r % 2
    x = xh * 2 + xl
    rows, cols = gout.shape
    quarter = rows // 4
    ntok = 4 * rows
    ngroups, members = mx.shape[1], mx.shape[2]
    nblocks = ntok // 128
    half_z = nz // 2

    def wrap(value, n):
        return lax.rem(value + 2 * n, n)

    def mate(m):
        other_h = 1 - xh if m & 2 else xh
        other_c = 1 - c if m & 1 else c
        return other_h * 2 + other_c

    def at_z(e):
        return (wrap(z + e, nz) * 4 + r, y, xl)

    def at_quad(m):
        return (z * 4 + mate(m), y, xl)

    def at_xy(axis, d):
        if axis == "y":
            return (dp, wrap(y + d, 4), xl)
        there = wrap(x + d, 4)
        return (z * 4 + (there // 2) * 2 + c, y, there % 2)

    def place(axis, first, second):
        dx, dy = (first, second) if axis == "x" else (second, first)
        px, py = wrap(x + dx, 4), wrap(y + dy, 4)
        return py * 2 + px % 2, px // 2

    msgs, tasks = {}, []

    def msg(name, src, dst, dev, link, nbytes, hops=1):
        msgs[name] = dict(src=src, dst=dst, dev=dev, link=link, bytes=nbytes, hops=hops, index=len(msgs))
        return name

    def task(name, deps=(), run=None, sends=(), cost=0.02, prio=5):
        tasks.append(dict(name=name, deps=list(deps), run=run, sends=list(sends), cost=cost, prio=prio))
        return name

    def copy_of(name):
        m = msgs[name]
        i = m["index"]
        return pltpu.make_async_remote_copy(
            src_ref=m["src"](), dst_ref=m["dst"](), send_sem=ssem.at[i], recv_sem=rsem.at[i],
            device_id=m["dev"](), device_id_type=MESH,
        )

    def lanes(block):
        return pl.ds(pl.multiple_of(block * 128, 128), 128)

    wbytes = 128 * 384 * 2
    for m in (1, 2, 3):
        link, hops = ("d", 1) if m == 1 else ("x2", 2)
        msg(("wq", m), lambda m=m: wst.at[mate(m)], lambda: wb.at[z, r], lambda m=m: at_quad(m), link, wbytes, hops)
        msg(("goq", m), lambda m=m: gout.at[:, lanes(mate(m))], lambda: go.at[r], lambda m=m: at_quad(m), link, rows * 256, hops)
    task("quad_w", sends=[("wq", 1), ("wq", 2), ("wq", 3)], prio=0)
    task("quad_go", deps=["quad_w", ("t2", 1, 0, 1)], sends=[("goq", 1), ("goq", 2), ("goq", 3)], prio=4)

    def reach(m, d):
        return half_z if (m < 2) == (d > 0) else half_z - 1

    for m in range(4):
        for d in SIGNS:
            for h in range(1, reach(m, d) + 1):
                where = lambda m=m, d=d, h=h: wb.at[wrap(z - d * (h - 1), nz), mate(m)]
                name = msg(("w", m, d, h), where, where, lambda d=d: at_z(d), "z+" if d > 0 else "z-", wbytes)
                if h > 1:
                    deps = [("w", m, d, h - 1)]
                else:
                    deps = [("wq", m)] if m else []
                task(("send", name), deps=deps, sends=[name], prio=0 if m < 2 else 1)

    hb, qb = 2 * quarter * cols * 2, quarter * cols * 2
    token_msgs = []
    for h in (0, 1):
        a1, a2 = ("x", "y") if h == 0 else ("y", "x")

        def piece(o, u, part, h=h, a1=a1):
            k, ph = place(a1, o, u)
            begin, size = {0: (0, 2), 1: (0, 1), -1: (1, 1)}[part]
            return tok.at[k, ph * 2 + c, pl.ds(h * 2 * quarter + begin * quarter, size * quarter), :]

        for d in SIGNS:
            w = lambda piece=piece: piece(0, 0, 0)
            msg(("t1", h, d), w, w, lambda a1=a1, d=d: at_xy(a1, d), a1 + "+-"[d < 0], hb)
            w = lambda piece=piece, d=d: piece(-d, 0, d)
            msg(("t1q", h, d), w, w, lambda a1=a1, d=d: at_xy(a1, d), a1 + "+-"[d < 0], qb)
            for o in (0, -1, 1, 2):
                w = lambda piece=piece, o=o: piece(o, 0, 0)
                msg(("t2", h, o, d), w, w, lambda a2=a2, d=d: at_xy(a2, d), a2 + "+-"[d < 0], hb)
                w = lambda piece=piece, o=o, d=d: piece(o, -d, d)
                msg(("t2q", h, o, d), w, w, lambda a2=a2, d=d: at_xy(a2, d), a2 + "+-"[d < 0], qb)
                token_msgs += [("t2", h, o, d), ("t2q", h, o, d)]
            token_msgs += [("t1", h, d), ("t1q", h, d)]
        for o in (0, -1, 1, 2):
            for u in (0, -1, 1, 2):
                w = lambda piece=piece, o=o, u=u: piece(o, u, 0)
                msg(("td", h, o, u), w, w, lambda: at_quad(1), "d", hb)
                token_msgs.append(("td", h, o, u))
        have = {0: [], -1: [("t1", h, 1)], 1: [("t1", h, -1)], 2: [("t1q", h, 1), ("t1q", h, -1)]}
        task(("tok1", h), deps=[], sends=[("t1", h, 1), ("t1", h, -1)], prio=0)
        for d in SIGNS:
            task(("tok1q", h, d), deps=[("t1", h, d)], sends=[("t1q", h, d)], prio=1)
        for o in (0, -1, 1, 2):
            task(("tok2", h, o), deps=have[o] + [("tok1", h)], sends=[("t2", h, o, 1), ("t2", h, o, -1)], prio=2)
            for d in SIGNS:
                task(("tok2q", h, o, d), deps=[("t2", h, o, d)], sends=[("t2q", h, o, d)], prio=2)
            there = {0: have[o], -1: [("t2", h, o, 1)], 1: [("t2", h, o, -1)], 2: [("t2q", h, o, 1), ("t2q", h, o, -1)]}
            for u in (0, -1, 1, 2):
                task(("tokd", h, o, u), deps=there[u], sends=[("td", h, o, u)], prio=3)
    task("tok_first", deps=[("tok1", 0), ("tok1", 1)], prio=0)
    task("tok_all", deps=token_msgs, prio=4)

    started = []

    def first_matmul(e, far):
        zs = wrap(z - e, nz)
        hf = 1 - xh if far else xh

        lhs = tok[zs, :, :, pl.ds(pl.multiple_of(hf * 256, 256), 256)].reshape(ntok, 256)
        rhs = wb[zs, pl.ds(hf * 2, 2)].reshape(256, 384)
        out = jnp.dot(lhs, rhs, preferred_element_type=F32)
        acc[...] = out + acc[...] if started else out
        started.append(e)

    mm = []
    for far in (False, True):
        for e in range(-half_z + 1, half_z + 1):
            pair = (2, 3) if far else (0, 1)
            if e == 0:
                deps = [("wq", m) for m in pair if m]
            elif e == half_z:
                d = -1 if far else 1
                deps = [("w", m, d, half_z) for m in pair]
            else:
                deps = [("w", m, 1 if e > 0 else -1, abs(e)) for m in pair]
            mm.append(task(("mm", e, far), deps=["tok_all"] + deps, run=lambda e=e, far=far: first_matmul(e, far), cost=0.45, prio=6))

    def build_toeplitz():
        for q in range(4):
            lfs[q] = lf[q * ngroups : (q + 1) * ngroups, :].astype(F32)
        for j in range(3):
            sfs[3 * j : 3 * j + 3, :] = sf[j, :, lanes(r)]

        def one(g, carry):
            row = lfs[r, pl.ds(g, 1), :]
            line = jnp.concatenate([row, jnp.zeros_like(row)], axis=1)
            skew = pltpu.roll(jnp.broadcast_to(line, (256, 256)), 0, 1, stride=1, stride_axis=0).astype(BF16)
            toe[g, 0:128, :] = skew[128:256, 0:128]
            toe[g, 128:256, :] = skew[0:128, 0:128]
            voe[g] = skew[0:128, :]
            return carry

        lax.fori_loop(0, ngroups, one, 0)
        sfs[...] = sfs[...].T

    task("toe", run=build_toeplitz, cost=3.0, prio=8)

    def turn_gout():
        flat = go[...].reshape(ntok, 128).T
        gox[:, :, 0:ntok] = flat.reshape(ngroups, members, ntok)

    msg("goh", lambda: gox.at[:, :, pl.ds(0, 256)], lambda: gox.at[:, :, pl.ds(ntok, 256)], lambda: at_z(-1), "z-", 128 * 512)
    task("got", deps=[("goq", 1), ("goq", 2), ("goq", 3)], run=turn_gout, sends=["goh"], cost=0.3, prio=3)

    def edge_rows():
        edge[0] = acc[0:144, :].astype(BF16)
        edge[1] = acc[ntok - 144 : ntok, :].astype(BF16)

    key, first = pl.ds(128, 256), pl.ds(0, 128)
    msg(("mh", 1, 1), lambda: edge.at[1, :, key], lambda: before.at[pl.ds(112, 144), key], lambda: at_z(1), "z+", 144 * 512)
    msg(("mh", 1, 0), lambda: edge.at[1, pl.ds(128, 16), first], lambda: before.at[pl.ds(240, 16), first], lambda: at_z(1), "z+", 16 * 256)
    msg(("mh", -1, 0), lambda: edge.at[0, :, first], lambda: after.at[pl.ds(0, 144), first], lambda: at_z(-1), "z-", 144 * 256)
    msg(("mh", -1, 1), lambda: edge.at[0, pl.ds(0, 16), key], lambda: after.at[pl.ds(0, 16), key], lambda: at_z(-1), "z-", 16 * 512)
    halos = [("mh", 1, 1), ("mh", 1, 0), ("mh", -1, 0), ("mh", -1, 1)]
    task("edge", deps=mm, run=edge_rows, sends=halos, cost=0.1, prio=0)

    def turn_mixed():
        for i in range(3):
            flat = acc[:, i * 128 : (i + 1) * 128].astype(BF16).T
            mx[i, :, :, 256 : 256 + ntok] = flat.reshape(ngroups, members, ntok)

    task("mxt", deps=["edge"], run=turn_mixed, cost=0.4, prio=0)

    def turn_halos():
        for i in range(3):
            for buf, off, dead in ((before, 0, z == 0), (after, 256 + ntok, z == nz - 1)):
                flat = buf[:, i * 128 : (i + 1) * 128].T
                mx[i, :, :, off : off + 256] = jnp.where(dead, jnp.zeros_like(flat), flat).reshape(ngroups, members, 256)
        ahead = gox[:, :, ntok : ntok + 256]
        gox[:, :, ntok : ntok + 256] = jnp.where(z == nz - 1, jnp.zeros_like(ahead), ahead)

    task("halo", deps=halos + ["goh", "mxt", "got"], run=turn_halos, cost=0.3, prio=0)

    span = ntok + 128

    def tap_of(g):
        taps = sfs[pl.ds(pl.multiple_of(g * members, members), members), :]
        return lambda j, i: taps[:, 3 * j + i : 3 * j + i + 1]

    def local_operator():
        def group(g, carry):
            tap = tap_of(g)
            feats = []
            for i in range(3):
                base = mx[i, g].astype(F32)
                feats.append(tap(0, i) * base + tap(1, i) * pltpu.roll(base, 1, 1) + tap(2, i) * pltpu.roll(base, 2, 1))
            product = (feats[1] * feats[2]).astype(BF16)
            pds[g] = product
            windows = jnp.concatenate([product[:, 128 * (b + 1) : 128 * (b + 3)] for b in range(nblocks + 1)], axis=0)
            out = jnp.dot(windows, toe[g], preferred_element_type=F32)
            conv = jnp.concatenate([out[members * b : members * (b + 1)] for b in range(nblocks + 1)], axis=1)
            up = gox[g].astype(F32)
            query = feats[0][:, 256:]
            gconv = (up * query).astype(BF16)
            gcs[g] = gconv[:, :ntok]
            ahead = jnp.concatenate([gconv[:, 128 * b : 128 * (b + 2)] for b in range(nblocks + 1)], axis=0)
            back = lax.dot_general(ahead, voe[g], (((1,), (1,)), ((), ())), preferred_element_type=F32)
            gproduct = jnp.concatenate([back[members * b : members * (b + 1)] for b in range(nblocks + 1)], axis=1)
            mxo[g] = (query[:, :ntok] * conv[:, :ntok]).astype(BF16)
            gfeats = [
                up[:, :span] * conv,
                gproduct * feats[2][:, 256 : 256 + span],
                gproduct * feats[1][:, 256 : 256 + span],
            ]
            for i in range(3):
                grad = tap(0, i) * gfeats[i] + tap(1, i) * pltpu.roll(gfeats[i], span - 1, 1) + tap(2, i) * pltpu.roll(gfeats[i], span - 2, 1)
                gmt[i, g] = grad[:, :ntok].astype(BF16)
                gfs[i, g] = gfeats[i][:, :ntok]
            return carry

        lax.fori_loop(0, ngroups, group, 0, unroll=UNROLL)

    task("local", deps=["halo", "toe"], run=local_operator, cost=4.5, prio=0)

    def flip_matrix():
        turned = lax.broadcasted_iota(jnp.int32, (128, 128), 0) + lax.broadcasted_iota(jnp.int32, (128, 128), 1) == 127
        return turned.astype(F32).astype(BF16)

    def filter_sums(part, size):
        lane = lax.broadcasted_iota(jnp.int32, (members, 128), 1)
        flip = flip_matrix()

        def group(n, carry):
            g = part * size + n
            sums = jnp.zeros((members, 128), F32)
            for i in range(3):
                base = mx[i, g, :, 128 : 256 + ntok].astype(F32)
                for j in range(3):
                    late = pltpu.roll(base, j, 1) if j else base
                    both = gfs[i, g] * late[:, 128:]
                    total = both[:, 0:128]
                    for b in range(1, nblocks):
                        total = total + both[:, 128 * b : 128 * (b + 1)]
                    sums = jnp.where(lane == 3 * j + i, jnp.sum(total, axis=1, keepdims=True), sums)
            gsb[pl.ds(pl.multiple_of(g * members, members), members), :] = sums
            windows = jnp.concatenate([pds[g, :, 128 * (b + 1) : 128 * (b + 3)] for b in range(nblocks)], axis=0)
            held = jnp.concatenate([gcs[g, :, 128 * b : 128 * (b + 1)] for b in range(nblocks)], axis=0)
            flipped = jnp.dot(held, flip, preferred_element_type=F32).astype(BF16)
            pairs = lax.dot_general(flipped, windows, (((0,), (0,)), ((), ())), preferred_element_type=F32)
            skew = pltpu.roll(pairs, 0, 1, stride=1, stride_axis=0)
            glb[pl.ds(g, 1), :] = jnp.sum(skew, axis=0, keepdims=True)[:, 128:]
            return carry

        lax.fori_loop(0, size, group, 0)

    def filter_pack():
        own_sums[0:8, :] = jnp.dot(glb[...].astype(BF16), flip_matrix(), preferred_element_type=F32)
        own_sums[8:24, :] = gsb[...].T[0:16, :]
        smv[...] = jnp.concatenate([own_sums[...], jnp.zeros((8, 128), F32)], axis=0).astype(BF16)

    parts = 4
    for n in range(parts):
        task(("sums", n), deps=["local"], run=lambda n=n: filter_sums(n, ngroups // parts), cost=0.8, prio=(3.21, 3.22, 3.28, 3.29)[n])

    for m in (1, 2, 3):
        link, hops = ("d", 1) if m == 1 else ("x2", 2)
        msg(
            ("mq", m), lambda m=m: mxt.at[pl.ds(pl.multiple_of(mate(m) * rows, rows), rows), :], lambda: mr.at[r],
            lambda m=m: at_quad(m), link, rows * 256, hops,
        )
        msg(("sq", m), lambda: smt, lambda m=m: sqr.at[m - 1], lambda m=m: at_quad(m), link, 24 * 512, hops)

    def turn_output():
        for g in range(ngroups):
            mxt[:, g * members : (g + 1) * members] = mxo[g].T

    task("mixed_send", deps=["local"], run=turn_output, sends=[("mq", m) for m in (1, 2, 3)], cost=0.3, prio=3.34)
    offsets = [e for e in range(-half_z + 1, half_z + 1) if e]
    for n, e in enumerate(offsets):
        msg(("sm", e), lambda: smv, lambda n=n: smr.at[n], lambda e=e: at_z(e), "z+" if e > 0 else "z-", 32 * 256, abs(e))
    task("small_send", deps=[("sums", n) for n in range(parts)], run=filter_pack, sends=[("sm", e) for e in offsets], cost=0.1, prio=3.295)

    def small_total():
        total = own_sums[...]
        for n in range(len(offsets)):
            total = total + smr[n, 0:24].astype(F32)
        smt[...] = total * scale

    task("small", deps=[("sm", e) for e in offsets] + ["small_send"], run=small_total, sends=[("sq", m) for m in (1, 2, 3)], cost=0.1, prio=1)

    def small_out():
        for m in range(4):
            part = smt[...] if m == 0 else sqr[m - 1]
            q = mate(m)
            gl_out[pl.ds(pl.multiple_of(q * 8, 8), 8), :] = part[0:8]
            for j in range(3):
                gs_out[j, :, lanes(q)] = part[8 + 3 * j : 11 + 3 * j]

    task("small_out", deps=[("sq", m) for m in (1, 2, 3)] + ["small"], run=small_out, cost=0.1, prio=9)

    def mixed_final():
        mixed_out[:, lanes(r)] = mxt[pl.ds(pl.multiple_of(r * rows, rows), rows), :]
        for m in (1, 2, 3):
            mixed_out[:, lanes(mate(m))] = mr[mate(m)]

    task("mixed_out", deps=[("mq", m) for m in (1, 2, 3)] + ["mixed_send"], run=mixed_final, cost=0.1, prio=9)

    def weight_partial(e):
        zc = wrap(z + e, nz)
        out = jnp.dot(gmt[...].reshape(384, ntok), tok[zc].reshape(ntok, cols), preferred_element_type=F32)
        for n in range(4):
            gp[e % nz, n] = out[:, n * 128 : (n + 1) * 128]

    chunks = [half_z]
    for e in range(half_z - 1, 0, -1):
        chunks += [e, -e]
    chunks.append(0)
    for n, e in enumerate(chunks):
        task(("gw", e % nz), deps=["local"], run=lambda e=e: weight_partial(e), cost=0.6, prio=3 + 0.05 * n)
    slot = {}
    for m in range(4):
        for d in SIGNS:
            top = reach(m, d)
            for h in range(top, 0, -1):
                slot[m, d, h] = len(slot)
    for m in (2, 3, 1, 0):
        for d in SIGNS:
            top = reach(m, d)
            for h in range(top, 0, -1):
                s = slot[m, d, h]
                name = msg(("wr", m, d, h), lambda s=s: ws.at[s], lambda s=s: wr.at[s], lambda d=d: at_z(d), "z+" if d > 0 else "z-", wbytes)
                deps = [("gw", (d * h) % nz)]
                if h < top:
                    deps.append(("wr", m, d, h + 1))
                elif m < 2:
                    deps += [("send", "wr", 2, d, 1), ("send", "wr", 3, d, 1)]

                def add(m=m, d=d, h=h, s=s, top=top):
                    value = gp[(d * h) % nz, mate(m)]
                    if h < top:
                        value = value + wr[slot[m, d, h + 1]].astype(F32)
                    ws[s] = value.astype(BF16)

                task(("send", "wr", m, d, h), deps=deps, run=add, sends=[name], cost=0.12, prio=0 if m >= 2 else 1)

    def weight_total(m):
        return (gp[0, mate(m)] + wr[slot[m, 1, 1]].astype(F32) + wr[slot[m, -1, 1]].astype(F32)) * scale

    def weight_store(m, value):
        for i in range(3):
            gw_out[i, :, lanes(mate(m))] = value[i * 128 : (i + 1) * 128, :].T

    for m in range(4):
        deps = [("gw", 0), ("wr", m, 1, 1), ("wr", m, -1, 1)]
        if m == 0:
            task("wtot0", deps=deps, run=lambda: weight_store(0, weight_total(0)), cost=0.5, prio=8)
            continue
        link, hops = ("d", 1) if m == 1 else ("x2", 2)
        msg(("wf", m), lambda m=m: fs.at[m - 1], lambda m=m: fr.at[m - 1], lambda m=m: at_quad(m), link, wbytes, hops)

        def finish(m=m):
            fs[m - 1] = weight_total(m).astype(BF16)

        task(("wtot", m), deps=deps, run=finish, sends=[("wf", m)], cost=0.2, prio=1)
        task(("wout", m), deps=[("wf", m)], run=lambda m=m: weight_store(m, fr[m - 1].astype(F32)), cost=0.5, prio=8)

    def feature_block(dy, dx):
        return wrap(y + dy, 4) * 2 + wrap(xl + dx, 2)

    def token_partial(dy, dx):
        k = feature_block(dy, dx)
        out = lax.dot_general(gm[...], wb[k].reshape(512, 384), (((1,), (1,)), ((), ())), preferred_element_type=F32)
        pp[k] = out.astype(BF16).reshape(4, rows, cols)

    def pair_sum(dy, dx):
        k = feature_block(dy, dx)
        for ph in range(2):
            pp[k, ph * 2 + c] = (pp[k, ph * 2 + c].astype(F32) + pr[k, ph].astype(F32)).astype(BF16)

    def turn_grad():
        for i in range(3):
            gm[:, i * 128 : (i + 1) * 128] = gmt[i].reshape(128, ntok).T

    task("turn_grad", deps=["local"], run=turn_grad, cost=0.3, prio=3.155)
    for n, dy in enumerate((2, 1, -1, 0)):
        for dx in (0, 1):
            both = [
                msg(
                    ("pd", dy, dx, ph), lambda dy=dy, dx=dx, ph=ph: pp.at[feature_block(dy, dx), ph * 2 + (1 - c)],
                    lambda dy=dy, dx=dx, ph=ph: pr.at[feature_block(dy, dx), ph], lambda: at_quad(1), "d", rows * cols * 2,
                )
                for ph in range(2)
            ]
            task(("pk", dy, dx), deps=["turn_grad"], run=lambda dy=dy, dx=dx: token_partial(dy, dx), sends=both, cost=0.75, prio=(3.16, 3.27, 3.31, 3.36)[n] + 0.01 * dx)
            task(("pa", dy, dx), deps=both + [("pk", dy, dx)], run=lambda dy=dy, dx=dx: pair_sum(dy, dx), cost=0.25, prio=2.5)

    def part_rows(h, part):
        begin, size = {0: (0, 2), 1: (0, 1), -1: (1, 1)}[part]
        return pl.ds(h * 2 * quarter + begin * quarter, size * quarter)

    def own_rows(part):
        return slice(0, quarter) if part > 0 else slice(quarter, 2 * quarter)

    for h in (0, 1):
        a1, a2 = ("y", "x") if h == 0 else ("x", "y")

        def needs(o1, o2, h=h):
            dy, dx = (o1, o2) if h == 0 else (o2, o1)
            dy = {0: 0, 1: 1, -1: -1, 2: 2}[dy]
            return ("pa", dy, dx % 2)

        def held(o1, o2, part, h=h, a1=a1):
            k, ph = place(a1, o1, o2)
            return pp.at[k, ph * 2 + c, part_rows(h, part), :]

        for o in (2, 1, -1, 0):
            oi = o % 4
            for d in SIGNS:
                di = 0 if d > 0 else 1
                link1 = a1 + "+-"[d < 0]
                msg(("s1q", h, o, d), lambda held=held, o=o, d=d: held(2, o, d), lambda h=h, oi=oi, di=di: q1.at[h, oi, di], lambda a1=a1, d=d: at_xy(a1, d), link1, qb)
                msg(("s1h", h, o, d), lambda h=h, oi=oi, di=di: h1s.at[h, oi, di], lambda h=h, oi=oi, di=di: h1.at[h, oi, di], lambda a1=a1, d=d: at_xy(a1, d), link1, hb)
                task(("s1q", h, o, d, "go"), deps=[needs(2, o)], sends=[("s1q", h, o, d)], prio=1)

                def forward(h=h, o=o, oi=oi, d=d, di=di, held=held):
                    own = held(d, o, 0)[...]
                    mine, rest = own_rows(d), own_rows(-d)
                    h1s[h, oi, di, mine, :] = (own[mine].astype(F32) + q1[h, oi, di].astype(F32)).astype(BF16)
                    h1s[h, oi, di, rest, :] = own[rest]

                task(("s1h", h, o, d, "go"), deps=[("s1q", h, o, d), needs(d, o)], run=forward, sends=[("s1h", h, o, d)], cost=0.08, prio=2)

            def settle(h=h, o=o, oi=oi, held=held):
                total = held(0, o, 0)[...].astype(F32) + h1[h, oi, 0].astype(F32) + h1[h, oi, 1].astype(F32)
                s1[h, oi] = total.astype(BF16)

            sends = []
            if o == 2:
                for d in SIGNS:
                    di = 0 if d > 0 else 1
                    part = slice(0, quarter) if d > 0 else slice(quarter, 2 * quarter)
                    begin = 0 if d > 0 else quarter
                    sends.append(
                        msg(("s2q", h, d), lambda h=h, begin=begin: s1.at[h, 2, pl.ds(begin, quarter), :], lambda h=h, di=di: q2.at[h, di], lambda a2=a2, d=d: at_xy(a2, d), a2 + "+-"[d < 0], qb)
                    )
            task(("s1", h, o), deps=[("s1h", h, o, 1), ("s1h", h, o, -1), needs(0, o)], run=settle, sends=sends, cost=0.08, prio=2)
        for d in SIGNS:
            di = 0 if d > 0 else 1
            msg(("s2h", h, d), lambda h=h, di=di: h2s.at[h, di], lambda h=h, di=di: h2.at[h, di], lambda a2=a2, d=d: at_xy(a2, d), a2 + "+-"[d < 0], hb)

            def second(h=h, d=d, di=di):
                own = s1[h, d % 4]
                mine, rest = own_rows(d), own_rows(-d)
                h2s[h, di, mine, :] = (own[mine].astype(F32) + q2[h, di].astype(F32)).astype(BF16)
                h2s[h, di, rest, :] = own[rest]

            task(("s2h", h, d, "go"), deps=[("s2q", h, d), ("s1", h, d)], run=second, sends=[("s2h", h, d)], cost=0.08, prio=2)

        def last(h=h):
            total = s1[h, 0].astype(F32) + h2[h, 0].astype(F32) + h2[h, 1].astype(F32)
            gin_out[h * 2 * quarter : (h + 1) * 2 * quarter, :] = total.astype(BF16)

        task(("gin", h), deps=[("s2h", h, 1), ("s2h", h, -1), ("s1", h, 0)], run=last, cost=0.1, prio=8)

    barrier = pltpu.get_barrier_semaphore()
    peers = [at_z(e) for e in SIGNS] + [at_quad(m) for m in (1, 2, 3)] + [at_xy(a, d) for a in ("x", "y") for d in SIGNS]
    for peer in peers:
        pl.semaphore_signal(barrier, inc=1, device_id=peer, device_id_type=MESH)
    k_me, _ = place("x", 0, 0)
    pairs = ((w3_hbm, w3), (tokens_hbm, tok.at[k_me, r]), (gout_hbm, gout), (sf_hbm, sf), (lf_hbm, lf))
    loads = [pltpu.make_async_copy(source, target, insem.at[n]) for n, (source, target) in enumerate(pairs)]
    for load in loads:
        load.start()
    before[...] = jnp.zeros_like(before)
    after[...] = jnp.zeros_like(after)
    loads[0].wait()
    for q in range(4):
        for i in range(3):
            wst[q, :, i * 128 : (i + 1) * 128] = w3[i, :, q * 128 : (q + 1) * 128]
    for i in range(3):
        wb[z, r, :, i * 128 : (i + 1) * 128] = w3[i, :, lanes(r)]
    for load in loads[1:]:
        load.wait()
    go[r] = gout[:, lanes(r)]
    sfs[...] = jnp.zeros_like(sfs)
    pl.semaphore_wait(barrier, len(peers))

    order, _ = planned_order(tasks, msgs)
    waited = set()
    for step in order:
        for dep in step["deps"]:
            if dep in msgs and dep not in waited:
                copy_of(dep).wait_recv()
                waited.add(dep)
        if step["run"] is not None:
            step["run"]()
        for name in step["sends"]:
            copy_of(name).start()
    for name in msgs:
        copy_of(name).wait_send()


def scratch(nz, rows, cols, n_messages):
    ntok = 4 * rows
    quarter = rows // 4
    v = pltpu.VMEM
    return [
        v((3, 128, cols), BF16),
        v((3, 3, cols), F32),
        v((32, 128), BF16),
        v((rows, cols), BF16),
        v((nz, 4, rows, cols), BF16),
        v((4, 128, 384), BF16),
        v((nz, 4, 128, 384), BF16),
        v((4, rows, 128), BF16),
        v((ntok, 384), F32),
        v((256, 384), BF16),
        v((256, 384), BF16),
        v((2, 144, 384), BF16),
        v((3, 8, 16, ntok + 512), BF16),
        v((8, 16, ntok + 256), BF16),
        v((8, 256, 128), BF16),
        v((8, 128, 256), BF16),
        v((4, 8, 128), F32),
        v((128, 128), F32),
        v((8, 16, ntok), BF16),
        v((ntok, 128), BF16),
        v((4, rows, 128), BF16),
        v((3, 8, 16, ntok), BF16),
        v((ntok, 384), BF16),
        v((8, 16, ntok), BF16),
        v((8, 16, ntok + 512), BF16),
        v((3, 8, 16, ntok), F32),
        v((8, 128), F32),
        v((128, 128), F32),
        v((24, 128), F32),
        v((32, 128), BF16),
        v((nz - 1, 32, 128), BF16),
        v((24, 128), F32),
        v((3, 24, 128), F32),
        v((nz, 4, 384, 128), F32),
        v((4 * (nz - 1), 384, 128), BF16),
        v((4 * (nz - 1), 384, 128), BF16),
        v((3, 384, 128), BF16),
        v((3, 384, 128), BF16),
        v((8, 4, rows, cols), BF16),
        v((8, 2, rows, cols), BF16),
        v((2, 4, 2, quarter, cols), BF16),
        v((2, 4, 2, 2 * quarter, cols), BF16),
        v((2, 4, 2, 2 * quarter, cols), BF16),
        v((2, 4, 2 * quarter, cols), BF16),
        v((2, 2, quarter, cols), BF16),
        v((2, 2, 2 * quarter, cols), BF16),
        v((2, 2, 2 * quarter, cols), BF16),
        pltpu.SemaphoreType.DMA((n_messages,)),
        pltpu.SemaphoreType.DMA((n_messages,)),
        pltpu.SemaphoreType.DMA((5,)),
    ]


def per_device(tokens, in_weight, short_filter, long_filter, grad_out):
    rows, cols = tokens.shape
    nz = lax.axis_size("dp") // 4
    scale = float(rows * 4 * nz) ** (-0.5)
    vmem = pl.BlockSpec(memory_space=pltpu.VMEM)

    def body(*refs):
        block_kernel(*refs, nz=nz, scale=scale)

    results = pl.pallas_call(
        body,
        out_shape=(
            pltpu.VMEM((rows, cols), BF16),
            pltpu.VMEM((rows, cols), BF16),
            pltpu.VMEM((3, 128, cols), F32),
            pltpu.VMEM((32, 128), F32),
            pltpu.VMEM((3, 3, cols), F32),
        ),
        in_specs=[pl.BlockSpec(memory_space=pl.ANY)] * 5,
        out_specs=(vmem,) * 5,
        scratch_shapes=scratch(nz, rows, cols, 256),
        compiler_params=pltpu.CompilerParams(
            collective_id=0, has_side_effects=True, vmem_limit_bytes=62 * 1024 * 1024
        ),
        name="hyena_block",
    )(tokens, in_weight.transpose(1, 0, 2), short_filter, long_filter, grad_out)

    def hand_over(*refs):
        sems = refs[-1]
        copies = [pltpu.make_async_copy(a, b, sems.at[n]) for n, (a, b) in enumerate(zip(refs[:5], refs[5:10]))]
        for copy in copies:
            copy.start()
        for copy in copies:
            copy.wait()

    mixed, grad_in, grad_w, grad_long, grad_short = pl.pallas_call(
        hand_over,
        out_shape=tuple(jax.ShapeDtypeStruct(a.shape, a.dtype) for a in results),
        in_specs=[vmem] * 5,
        out_specs=(pl.BlockSpec(memory_space=pl.ANY),) * 5,
        scratch_shapes=[pltpu.SemaphoreType.DMA((5,))],
        name="hand_over",
    )(*[pltpu.with_memory_space_constraint(a, pltpu.VMEM) for a in results])
    return mixed, grad_in, grad_w.transpose(1, 0, 2), grad_long, grad_short


def solution(mesh):
    placed = (
        P("dp", ("row", "col")),
        P("dp", None, ("row", "col")),
        P(None, None, ("row", "col")),
        P(("row", "col"), None),
        P("dp", ("row", "col")),
    )
    return jax.shard_map(
        per_device,
        mesh=mesh,
        in_specs=placed,
        out_specs=(
            P("dp", ("row", "col")),
            P("dp", ("row", "col")),
            P("dp", None, ("row", "col")),
            P(("row", "col"), None),
            P(None, None, ("row", "col")),
        ),
        check_vma=False,
    )
```

```python
import jax
import jax.numpy as jnp
from jax import lax
from jax.experimental import pallas as pl
from jax.experimental.pallas import tpu as pltpu
from jax.sharding import PartitionSpec as P

MESH = pl.DeviceIdType.MESH
F32, BF16 = jnp.float32, jnp.bfloat16
SIGNS = (1, -1)
UNROLL = 1

ORDER = (
    30, 2, 6, 0, 33, 67, 61, 64, 92, 110, 13, 9, 32, 40, 43, 50, 34, 38, 37, 35, 7, 47, 31, 3,
    36, 78, 62, 81, 63, 71, 74, 14, 16, 19, 10, 44, 42, 41, 45, 39, 8, 23, 26, 4, 1, 66, 68, 69,
    65, 54, 57, 48, 49, 52, 15, 17, 51, 85, 88, 80, 82, 79, 83, 46, 20, 11, 75, 76, 73, 72, 59, 56,
    55, 58, 24, 53, 27, 5, 70, 60, 111, 18, 87, 86, 90, 89, 84, 21, 12, 77, 91, 28, 25, 93, 105, 107,
    94, 22, 103, 95, 104, 29, 96, 101, 100, 102, 98, 106, 99, 108, 97, 109, 112, 113, 114, 115, 127, 125, 151, 130,
    148, 131, 120, 141, 176, 144, 117, 119, 135, 129, 152, 149, 118, 133, 177, 142, 145, 189, 132, 128, 178, 218, 210, 150,
    216, 153, 195, 193, 190, 231, 181, 143, 146, 137, 179, 233, 126, 182, 223, 155, 154, 162, 221, 185, 180, 205, 200, 203,
    217, 219, 198, 147, 159, 166, 194, 139, 186, 228, 226, 134, 156, 116, 121, 174, 183, 220, 172, 163, 136, 196, 187, 157,
    184, 199, 222, 204, 224, 160, 191, 188, 206, 229, 167, 227, 197, 164, 201, 138, 192, 232, 234, 140, 208, 225, 236, 158,
    161, 173, 211, 122, 207, 124, 230, 237, 165, 168, 209, 239, 214, 202, 213, 175, 170, 235, 171, 169, 212, 123, 238, 215,
)


def block_kernel(
    tokens_hbm, w3_hbm, sf_hbm, lf_hbm, gout_hbm, mixed_out, gin_out, gw_out, gl_out, gs_out,
    w3, sf, lf, gout, tok, wst, wb, go, acc, before, after, edge, mx, gox, toe, voe, lfs, sfs, mxo, mxt, mr, gmt, gm,
    gcs, pds, gfs, glb, gsb, own_sums, smv, smr, smt, sqr, gp, ws, wr, fs, fr, pp, pr, q1, h1s, h1, s1, q2, h2s, h2,
    ssem, rsem, insem, *, nz, scale,
):
    dp, y, xl = lax.axis_index("dp"), lax.axis_index("row"), lax.axis_index("col")
    z, r = dp // 4, dp % 4
    xh, c = r // 2, r % 2
    x = xh * 2 + xl
    rows, cols = gout.shape
    quarter = rows // 4
    ntok = 4 * rows
    ngroups, members = mx.shape[1], mx.shape[2]
    nblocks = ntok // 128
    half_z = nz // 2

    def wrap(value, n):
        return lax.rem(value + 2 * n, n)

    def mate(m):
        other_h = 1 - xh if m & 2 else xh
        other_c = 1 - c if m & 1 else c
        return other_h * 2 + other_c

    def at_z(e):
        return (wrap(z + e, nz) * 4 + r, y, xl)

    def at_quad(m):
        return (z * 4 + mate(m), y, xl)

    def at_xy(axis, d):
        if axis == "y":
            return (dp, wrap(y + d, 4), xl)
        there = wrap(x + d, 4)
        return (z * 4 + (there // 2) * 2 + c, y, there % 2)

    def place(axis, first, second):
        dx, dy = (first, second) if axis == "x" else (second, first)
        px, py = wrap(x + dx, 4), wrap(y + dy, 4)
        return py * 2 + px % 2, px // 2

    msgs, tasks = {}, []

    def msg(name, src, dst, dev, link, nbytes, hops=1):
        msgs[name] = dict(src=src, dst=dst, dev=dev, link=link, bytes=nbytes, hops=hops, index=len(msgs))
        return name

    def task(name, deps=(), run=None, sends=(), cost=0.02, prio=5):
        tasks.append(dict(name=name, deps=list(deps), run=run, sends=list(sends), cost=cost, prio=prio))
        return name

    def copy_of(name):
        m = msgs[name]
        i = m["index"]
        return pltpu.make_async_remote_copy(
            src_ref=m["src"](), dst_ref=m["dst"](), send_sem=ssem.at[i], recv_sem=rsem.at[i],
            device_id=m["dev"](), device_id_type=MESH,
        )

    def lanes(block):
        return pl.ds(pl.multiple_of(block * 128, 128), 128)

    wbytes = 128 * 384 * 2
    for m in (1, 2, 3):
        link, hops = ("d", 1) if m == 1 else ("x2", 2)
        msg(("wq", m), lambda m=m: wst.at[mate(m)], lambda: wb.at[z, r], lambda m=m: at_quad(m), link, wbytes, hops)
        msg(("goq", m), lambda m=m: gout.at[:, lanes(mate(m))], lambda: go.at[r], lambda m=m: at_quad(m), link, rows * 256, hops)
    task("quad_w", sends=[("wq", 1), ("wq", 2), ("wq", 3)], prio=0)
    task("quad_go", deps=["quad_w", ("t2", 1, 0, 1)], sends=[("goq", 1), ("goq", 2), ("goq", 3)], prio=4)

    def reach(m, d):
        return half_z if (m < 2) == (d > 0) else half_z - 1

    for m in range(4):
        for d in SIGNS:
            for h in range(1, reach(m, d) + 1):
                where = lambda m=m, d=d, h=h: wb.at[wrap(z - d * (h - 1), nz), mate(m)]
                name = msg(("w", m, d, h), where, where, lambda d=d: at_z(d), "z+" if d > 0 else "z-", wbytes)
                if h > 1:
                    deps = [("w", m, d, h - 1)]
                else:
                    deps = [("wq", m)] if m else []
                task(("send", name), deps=deps, sends=[name], prio=0 if m < 2 else 1)

    hb, qb = 2 * quarter * cols * 2, quarter * cols * 2
    token_msgs = []
    for h in (0, 1):
        a1, a2 = ("x", "y") if h == 0 else ("y", "x")

        def piece(o, u, part, h=h, a1=a1):
            k, ph = place(a1, o, u)
            begin, size = {0: (0, 2), 1: (0, 1), -1: (1, 1)}[part]
            return tok.at[k, ph * 2 + c, pl.ds(h * 2 * quarter + begin * quarter, size * quarter), :]

        for d in SIGNS:
            w = lambda piece=piece: piece(0, 0, 0)
            msg(("t1", h, d), w, w, lambda a1=a1, d=d: at_xy(a1, d), a1 + "+-"[d < 0], hb)
            w = lambda piece=piece, d=d: piece(-d, 0, d)
            msg(("t1q", h, d), w, w, lambda a1=a1, d=d: at_xy(a1, d), a1 + "+-"[d < 0], qb)
            for o in (0, -1, 1, 2):
                w = lambda piece=piece, o=o: piece(o, 0, 0)
                msg(("t2", h, o, d), w, w, lambda a2=a2, d=d: at_xy(a2, d), a2 + "+-"[d < 0], hb)
                w = lambda piece=piece, o=o, d=d: piece(o, -d, d)
                msg(("t2q", h, o, d), w, w, lambda a2=a2, d=d: at_xy(a2, d), a2 + "+-"[d < 0], qb)
                token_msgs += [("t2", h, o, d), ("t2q", h, o, d)]
            token_msgs += [("t1", h, d), ("t1q", h, d)]
        for o in (0, -1, 1, 2):
            for u in (0, -1, 1, 2):
                w = lambda piece=piece, o=o, u=u: piece(o, u, 0)
                msg(("td", h, o, u), w, w, lambda: at_quad(1), "d", hb)
                token_msgs.append(("td", h, o, u))
        have = {0: [], -1: [("t1", h, 1)], 1: [("t1", h, -1)], 2: [("t1q", h, 1), ("t1q", h, -1)]}
        task(("tok1", h), deps=[], sends=[("t1", h, 1), ("t1", h, -1)], prio=0)
        for d in SIGNS:
            task(("tok1q", h, d), deps=[("t1", h, d)], sends=[("t1q", h, d)], prio=1)
        for o in (0, -1, 1, 2):
            task(("tok2", h, o), deps=have[o] + [("tok1", h)], sends=[("t2", h, o, 1), ("t2", h, o, -1)], prio=2)
            for d in SIGNS:
                task(("tok2q", h, o, d), deps=[("t2", h, o, d)], sends=[("t2q", h, o, d)], prio=2)
            there = {0: have[o], -1: [("t2", h, o, 1)], 1: [("t2", h, o, -1)], 2: [("t2q", h, o, 1), ("t2q", h, o, -1)]}
            for u in (0, -1, 1, 2):
                task(("tokd", h, o, u), deps=there[u], sends=[("td", h, o, u)], prio=3)
    task("tok_first", deps=[("tok1", 0), ("tok1", 1)], prio=0)
    task("tok_all", deps=token_msgs, prio=4)

    started = []

    def first_matmul(e, far):
        zs = wrap(z - e, nz)
        hf = 1 - xh if far else xh

        lhs = tok[zs, :, :, pl.ds(pl.multiple_of(hf * 256, 256), 256)].reshape(ntok, 256)
        rhs = wb[zs, pl.ds(hf * 2, 2)].reshape(256, 384)
        out = jnp.dot(lhs, rhs, preferred_element_type=F32)
        acc[...] = out + acc[...] if started else out
        started.append(e)

    mm = []
    for far in (False, True):
        for e in range(-half_z + 1, half_z + 1):
            pair = (2, 3) if far else (0, 1)
            if e == 0:
                deps = [("wq", m) for m in pair if m]
            elif e == half_z:
                d = -1 if far else 1
                deps = [("w", m, d, half_z) for m in pair]
            else:
                deps = [("w", m, 1 if e > 0 else -1, abs(e)) for m in pair]
            mm.append(task(("mm", e, far), deps=["tok_all"] + deps, run=lambda e=e, far=far: first_matmul(e, far), cost=0.45, prio=6))

    def build_toeplitz():
        for q in range(4):
            lfs[q] = lf[q * ngroups : (q + 1) * ngroups, :].astype(F32)
        for j in range(3):
            sfs[3 * j : 3 * j + 3, :] = sf[j, :, lanes(r)]

        def one(g, carry):
            row = lfs[r, pl.ds(g, 1), :]
            line = jnp.concatenate([row, jnp.zeros_like(row)], axis=1)
            skew = pltpu.roll(jnp.broadcast_to(line, (256, 256)), 0, 1, stride=1, stride_axis=0).astype(BF16)
            toe[g, 0:128, :] = skew[128:256, 0:128]
            toe[g, 128:256, :] = skew[0:128, 0:128]
            voe[g] = skew[0:128, :]
            return carry

        lax.fori_loop(0, ngroups, one, 0)
        sfs[...] = sfs[...].T

    task("toe", run=build_toeplitz, cost=3.0, prio=8)

    def turn_gout():
        flat = go[...].reshape(ntok, 128).T
        gox[:, :, 0:ntok] = flat.reshape(ngroups, members, ntok)

    msg(("goh",), lambda: gox.at[:, :, pl.ds(0, 256)], lambda: gox.at[:, :, pl.ds(ntok, 256)], lambda: at_z(-1), "z-", 128 * 512)
    task("got", deps=[("goq", 1), ("goq", 2), ("goq", 3)], run=turn_gout, sends=[("goh",)], cost=0.3, prio=3)

    def edge_rows():
        edge[0] = acc[0:144, :].astype(BF16)
        edge[1] = acc[ntok - 144 : ntok, :].astype(BF16)

    key, first = pl.ds(128, 256), pl.ds(0, 128)
    msg(("mh", 1, 1), lambda: edge.at[1, :, key], lambda: before.at[pl.ds(112, 144), key], lambda: at_z(1), "z+", 144 * 512)
    msg(("mh", 1, 0), lambda: edge.at[1, pl.ds(128, 16), first], lambda: before.at[pl.ds(240, 16), first], lambda: at_z(1), "z+", 16 * 256)
    msg(("mh", -1, 0), lambda: edge.at[0, :, first], lambda: after.at[pl.ds(0, 144), first], lambda: at_z(-1), "z-", 144 * 256)
    msg(("mh", -1, 1), lambda: edge.at[0, pl.ds(0, 16), key], lambda: after.at[pl.ds(0, 16), key], lambda: at_z(-1), "z-", 16 * 512)
    halos = [("mh", 1, 1), ("mh", 1, 0), ("mh", -1, 0), ("mh", -1, 1)]
    task("edge", deps=mm, run=edge_rows, sends=halos, cost=0.1, prio=0)

    def turn_mixed():
        for i in range(3):
            flat = acc[:, i * 128 : (i + 1) * 128].astype(BF16).T
            mx[i, :, :, 256 : 256 + ntok] = flat.reshape(ngroups, members, ntok)

    task("mxt", deps=["edge"], run=turn_mixed, cost=0.4, prio=0)

    def turn_halos():
        for i in range(3):
            for buf, off, dead in ((before, 0, z == 0), (after, 256 + ntok, z == nz - 1)):
                flat = buf[:, i * 128 : (i + 1) * 128].T
                mx[i, :, :, off : off + 256] = jnp.where(dead, jnp.zeros_like(flat), flat).reshape(ngroups, members, 256)
        ahead = gox[:, :, ntok : ntok + 256]
        gox[:, :, ntok : ntok + 256] = jnp.where(z == nz - 1, jnp.zeros_like(ahead), ahead)

    task("halo", deps=halos + [("goh",), "mxt", "got"], run=turn_halos, cost=0.3, prio=0)

    span = ntok + 128

    def tap_of(g):
        taps = sfs[pl.ds(pl.multiple_of(g * members, members), members), :]
        return lambda j, i: taps[:, 3 * j + i : 3 * j + i + 1]

    def local_operator():
        def group(g, carry):
            tap = tap_of(g)
            feats = []
            for i in range(3):
                base = mx[i, g].astype(F32)
                feats.append(tap(0, i) * base + tap(1, i) * pltpu.roll(base, 1, 1) + tap(2, i) * pltpu.roll(base, 2, 1))
            product = (feats[1] * feats[2]).astype(BF16)
            pds[g] = product
            windows = jnp.concatenate([product[:, 128 * (b + 1) : 128 * (b + 3)] for b in range(nblocks + 1)], axis=0)
            out = jnp.dot(windows, toe[g], preferred_element_type=F32)
            conv = jnp.concatenate([out[members * b : members * (b + 1)] for b in range(nblocks + 1)], axis=1)
            up = gox[g].astype(F32)
            query = feats[0][:, 256:]
            gconv = (up * query).astype(BF16)
            gcs[g] = gconv[:, :ntok]
            ahead = jnp.concatenate([gconv[:, 128 * b : 128 * (b + 2)] for b in range(nblocks + 1)], axis=0)
            back = lax.dot_general(ahead, voe[g], (((1,), (1,)), ((), ())), preferred_element_type=F32)
            gproduct = jnp.concatenate([back[members * b : members * (b + 1)] for b in range(nblocks + 1)], axis=1)
            mxo[g] = (query[:, :ntok] * conv[:, :ntok]).astype(BF16)
            gfeats = [
                up[:, :span] * conv,
                gproduct * feats[2][:, 256 : 256 + span],
                gproduct * feats[1][:, 256 : 256 + span],
            ]
            for i in range(3):
                grad = tap(0, i) * gfeats[i] + tap(1, i) * pltpu.roll(gfeats[i], span - 1, 1) + tap(2, i) * pltpu.roll(gfeats[i], span - 2, 1)
                gmt[i, g] = grad[:, :ntok].astype(BF16)
                gfs[i, g] = gfeats[i][:, :ntok]
            return carry

        lax.fori_loop(0, ngroups, group, 0, unroll=UNROLL)

    task("local", deps=["halo", "toe"], run=local_operator, cost=4.5, prio=0)

    def flip_matrix():
        turned = lax.broadcasted_iota(jnp.int32, (128, 128), 0) + lax.broadcasted_iota(jnp.int32, (128, 128), 1) == 127
        return turned.astype(F32).astype(BF16)

    def filter_sums(part, size):
        lane = lax.broadcasted_iota(jnp.int32, (members, 128), 1)
        flip = flip_matrix()

        def group(n, carry):
            g = part * size + n
            sums = jnp.zeros((members, 128), F32)
            for i in range(3):
                base = mx[i, g, :, 128 : 256 + ntok].astype(F32)
                for j in range(3):
                    late = pltpu.roll(base, j, 1) if j else base
                    both = gfs[i, g] * late[:, 128:]
                    total = both[:, 0:128]
                    for b in range(1, nblocks):
                        total = total + both[:, 128 * b : 128 * (b + 1)]
                    sums = jnp.where(lane == 3 * j + i, jnp.sum(total, axis=1, keepdims=True), sums)
            gsb[pl.ds(pl.multiple_of(g * members, members), members), :] = sums
            windows = jnp.concatenate([pds[g, :, 128 * (b + 1) : 128 * (b + 3)] for b in range(nblocks)], axis=0)
            held = jnp.concatenate([gcs[g, :, 128 * b : 128 * (b + 1)] for b in range(nblocks)], axis=0)
            flipped = jnp.dot(held, flip, preferred_element_type=F32).astype(BF16)
            pairs = lax.dot_general(flipped, windows, (((0,), (0,)), ((), ())), preferred_element_type=F32)
            skew = pltpu.roll(pairs, 0, 1, stride=1, stride_axis=0)
            glb[pl.ds(g, 1), :] = jnp.sum(skew, axis=0, keepdims=True)[:, 128:]
            return carry

        lax.fori_loop(0, size, group, 0)

    def filter_pack():
        own_sums[0:8, :] = jnp.dot(glb[...].astype(BF16), flip_matrix(), preferred_element_type=F32)
        own_sums[8:24, :] = gsb[...].T[0:16, :]
        smv[...] = jnp.concatenate([own_sums[...], jnp.zeros((8, 128), F32)], axis=0).astype(BF16)

    parts = 4
    for n in range(parts):
        task(("sums", n), deps=["local"], run=lambda n=n: filter_sums(n, ngroups // parts), cost=0.8, prio=(3.21, 3.22, 3.28, 3.29)[n])

    for m in (1, 2, 3):
        link, hops = ("d", 1) if m == 1 else ("x2", 2)
        msg(
            ("mq", m), lambda m=m: mxt.at[pl.ds(pl.multiple_of(mate(m) * rows, rows), rows), :], lambda: mr.at[r],
            lambda m=m: at_quad(m), link, rows * 256, hops,
        )
        msg(("sq", m), lambda: smt, lambda m=m: sqr.at[m - 1], lambda m=m: at_quad(m), link, 24 * 512, hops)

    def turn_output():
        for g in range(ngroups):
            mxt[:, g * members : (g + 1) * members] = mxo[g].T

    task("mixed_send", deps=["local"], run=turn_output, sends=[("mq", m) for m in (1, 2, 3)], cost=0.3, prio=3.34)
    offsets = [e for e in range(-half_z + 1, half_z + 1) if e]
    for n, e in enumerate(offsets):
        msg(("sm", e), lambda: smv, lambda n=n: smr.at[n], lambda e=e: at_z(e), "z+" if e > 0 else "z-", 32 * 256, abs(e))
    task("small_send", deps=[("sums", n) for n in range(parts)], run=filter_pack, sends=[("sm", e) for e in offsets], cost=0.1, prio=3.295)

    def small_total():
        total = own_sums[...]
        for n in range(len(offsets)):
            total = total + smr[n, 0:24].astype(F32)
        smt[...] = total * scale

    task("small", deps=[("sm", e) for e in offsets] + ["small_send"], run=small_total, sends=[("sq", m) for m in (1, 2, 3)], cost=0.1, prio=1)

    def small_out():
        for m in range(4):
            part = smt[...] if m == 0 else sqr[m - 1]
            q = mate(m)
            gl_out[pl.ds(pl.multiple_of(q * 8, 8), 8), :] = part[0:8]
            for j in range(3):
                gs_out[j, :, lanes(q)] = part[8 + 3 * j : 11 + 3 * j]

    task("small_out", deps=[("sq", m) for m in (1, 2, 3)] + ["small"], run=small_out, cost=0.1, prio=9)

    def mixed_final():
        mixed_out[:, lanes(r)] = mxt[pl.ds(pl.multiple_of(r * rows, rows), rows), :]
        for m in (1, 2, 3):
            mixed_out[:, lanes(mate(m))] = mr[mate(m)]

    task("mixed_out", deps=[("mq", m) for m in (1, 2, 3)] + ["mixed_send"], run=mixed_final, cost=0.1, prio=9)

    def weight_partial(e, far):
        zc = wrap(z + e, nz)
        hf = 1 - xh if far else xh
        rhs = tok[zc, :, :, pl.ds(pl.multiple_of(hf * 256, 256), 256)].reshape(ntok, 256)
        out = jnp.dot(gmt[...].reshape(384, ntok), rhs, preferred_element_type=F32)
        for n in range(2):
            gp[e % nz, hf * 2 + n] = out[:, n * 128 : (n + 1) * 128]

    chunks = [half_z]
    for e in range(half_z - 1, 0, -1):
        chunks += [e, -e]
    chunks.append(0)
    for n, e in enumerate(chunks):
        for far in (True, False):
            task(
                ("gw", e % nz, far), deps=["local"], run=lambda e=e, far=far: weight_partial(e, far), cost=0.38,
                prio=3 + 0.05 * n + (0 if far else 0.02),
            )
    slot = {}
    for m in range(4):
        for d in SIGNS:
            top = reach(m, d)
            for h in range(top, 0, -1):
                slot[m, d, h] = len(slot)
    for m in (2, 3, 1, 0):
        for d in SIGNS:
            top = reach(m, d)
            for h in range(top, 0, -1):
                s = slot[m, d, h]
                name = msg(("wr", m, d, h), lambda s=s: ws.at[s], lambda s=s: wr.at[s], lambda d=d: at_z(d), "z+" if d > 0 else "z-", wbytes)
                deps = [("gw", (d * h) % nz, m >= 2)]
                if h < top:
                    deps.append(("wr", m, d, h + 1))
                elif m < 2:
                    deps += [("send", "wr", 2, d, 1), ("send", "wr", 3, d, 1)]

                def add(m=m, d=d, h=h, s=s, top=top):
                    value = gp[(d * h) % nz, mate(m)]
                    if h < top:
                        value = value + wr[slot[m, d, h + 1]].astype(F32)
                    ws[s] = value.astype(BF16)

                task(("send", "wr", m, d, h), deps=deps, run=add, sends=[name], cost=0.12, prio=0 if m >= 2 else 1)

    def weight_total(m):
        return (gp[0, mate(m)] + wr[slot[m, 1, 1]].astype(F32) + wr[slot[m, -1, 1]].astype(F32)) * scale

    def weight_store(m, value):
        for i in range(3):
            gw_out[i, :, lanes(mate(m))] = value[i * 128 : (i + 1) * 128, :].T

    for m in range(4):
        deps = [("gw", 0, m >= 2), ("wr", m, 1, 1), ("wr", m, -1, 1)]
        if m == 0:
            task("wtot0", deps=deps, run=lambda: weight_store(0, weight_total(0)), cost=0.5, prio=8)
            continue
        link, hops = ("d", 1) if m == 1 else ("x2", 2)
        msg(("wf", m), lambda m=m: fs.at[m - 1], lambda m=m: fr.at[m - 1], lambda m=m: at_quad(m), link, wbytes, hops)

        def finish(m=m):
            fs[m - 1] = weight_total(m).astype(BF16)

        task(("wtot", m), deps=deps, run=finish, sends=[("wf", m)], cost=0.2, prio=1)
        task(("wout", m), deps=[("wf", m)], run=lambda m=m: weight_store(m, fr[m - 1].astype(F32)), cost=0.5, prio=8)

    def feature_block(dy, dx):
        return wrap(y + dy, 4) * 2 + wrap(xl + dx, 2)

    def token_partial(dy, dx):
        k = feature_block(dy, dx)
        out = lax.dot_general(gm[...], wb[k].reshape(512, 384), (((1,), (1,)), ((), ())), preferred_element_type=F32)
        pp[k] = out.astype(BF16).reshape(4, rows, cols)

    def pair_sum(dy, dx):
        k = feature_block(dy, dx)
        for ph in range(2):
            pp[k, ph * 2 + c] = (pp[k, ph * 2 + c].astype(F32) + pr[k, ph].astype(F32)).astype(BF16)

    def turn_grad():
        for i in range(3):
            gm[:, i * 128 : (i + 1) * 128] = gmt[i].reshape(128, ntok).T

    task("turn_grad", deps=["local"], run=turn_grad, cost=0.3, prio=3.155)
    for n, dy in enumerate((2, 1, -1, 0)):
        for dx in (0, 1):
            both = [
                msg(
                    ("pd", dy, dx, ph), lambda dy=dy, dx=dx, ph=ph: pp.at[feature_block(dy, dx), ph * 2 + (1 - c)],
                    lambda dy=dy, dx=dx, ph=ph: pr.at[feature_block(dy, dx), ph], lambda: at_quad(1), "d", rows * cols * 2,
                )
                for ph in range(2)
            ]
            task(("pk", dy, dx), deps=["turn_grad"], run=lambda dy=dy, dx=dx: token_partial(dy, dx), sends=both, cost=0.75, prio=(3.16, 3.27, 3.31, 3.36)[n] + 0.01 * dx)
            task(("pa", dy, dx), deps=both + [("pk", dy, dx)], run=lambda dy=dy, dx=dx: pair_sum(dy, dx), cost=0.25, prio=2.5)

    def part_rows(h, part):
        begin, size = {0: (0, 2), 1: (0, 1), -1: (1, 1)}[part]
        return pl.ds(h * 2 * quarter + begin * quarter, size * quarter)

    def own_rows(part):
        return slice(0, quarter) if part > 0 else slice(quarter, 2 * quarter)

    for h in (0, 1):
        a1, a2 = ("y", "x") if h == 0 else ("x", "y")

        def needs(o1, o2, h=h):
            dy, dx = (o1, o2) if h == 0 else (o2, o1)
            dy = {0: 0, 1: 1, -1: -1, 2: 2}[dy]
            return ("pa", dy, dx % 2)

        def held(o1, o2, part, h=h, a1=a1):
            k, ph = place(a1, o1, o2)
            return pp.at[k, ph * 2 + c, part_rows(h, part), :]

        for o in (2, 1, -1, 0):
            oi = o % 4
            for d in SIGNS:
                di = 0 if d > 0 else 1
                link1 = a1 + "+-"[d < 0]
                msg(("s1q", h, o, d), lambda held=held, o=o, d=d: held(2, o, d), lambda h=h, oi=oi, di=di: q1.at[h, oi, di], lambda a1=a1, d=d: at_xy(a1, d), link1, qb)
                msg(("s1h", h, o, d), lambda h=h, oi=oi, di=di: h1s.at[h, oi, di], lambda h=h, oi=oi, di=di: h1.at[h, oi, di], lambda a1=a1, d=d: at_xy(a1, d), link1, hb)
                task(("s1q", h, o, d, "go"), deps=[needs(2, o)], sends=[("s1q", h, o, d)], prio=1)

                def forward(h=h, o=o, oi=oi, d=d, di=di, held=held):
                    own = held(d, o, 0)[...]
                    mine, rest = own_rows(d), own_rows(-d)
                    h1s[h, oi, di, mine, :] = (own[mine].astype(F32) + q1[h, oi, di].astype(F32)).astype(BF16)
                    h1s[h, oi, di, rest, :] = own[rest]

                task(("s1h", h, o, d, "go"), deps=[("s1q", h, o, d), needs(d, o)], run=forward, sends=[("s1h", h, o, d)], cost=0.08, prio=2)

            def settle(h=h, o=o, oi=oi, held=held):
                total = held(0, o, 0)[...].astype(F32) + h1[h, oi, 0].astype(F32) + h1[h, oi, 1].astype(F32)
                s1[h, oi] = total.astype(BF16)

            sends = []
            if o == 2:
                for d in SIGNS:
                    di = 0 if d > 0 else 1
                    part = slice(0, quarter) if d > 0 else slice(quarter, 2 * quarter)
                    begin = 0 if d > 0 else quarter
                    sends.append(
                        msg(("s2q", h, d), lambda h=h, begin=begin: s1.at[h, 2, pl.ds(begin, quarter), :], lambda h=h, di=di: q2.at[h, di], lambda a2=a2, d=d: at_xy(a2, d), a2 + "+-"[d < 0], qb)
                    )
            task(("s1", h, o), deps=[("s1h", h, o, 1), ("s1h", h, o, -1), needs(0, o)], run=settle, sends=sends, cost=0.08, prio=2)
        for d in SIGNS:
            di = 0 if d > 0 else 1
            msg(("s2h", h, d), lambda h=h, di=di: h2s.at[h, di], lambda h=h, di=di: h2.at[h, di], lambda a2=a2, d=d: at_xy(a2, d), a2 + "+-"[d < 0], hb)

            def second(h=h, d=d, di=di):
                own = s1[h, d % 4]
                mine, rest = own_rows(d), own_rows(-d)
                h2s[h, di, mine, :] = (own[mine].astype(F32) + q2[h, di].astype(F32)).astype(BF16)
                h2s[h, di, rest, :] = own[rest]

            task(("s2h", h, d, "go"), deps=[("s2q", h, d), ("s1", h, d)], run=second, sends=[("s2h", h, d)], cost=0.08, prio=2)

        def last(h=h):
            total = s1[h, 0].astype(F32) + h2[h, 0].astype(F32) + h2[h, 1].astype(F32)
            gin_out[h * 2 * quarter : (h + 1) * 2 * quarter, :] = total.astype(BF16)

        task(("gin", h), deps=[("s2h", h, 1), ("s2h", h, -1), ("s1", h, 0)], run=last, cost=0.1, prio=8)

    sent = set()

    def drain(kinds):
        for name in msgs:
            if name not in sent and name[0] in kinds:
                copy_of(name).wait_send()
                sent.add(name)

    first_half = ("wq", "goq", "w", "t1", "t1q", "t2", "t2q", "td", "goh", "mh", "g")
    task("drain1", deps=["mixed_out"], run=lambda: drain(first_half), cost=0.6, prio=9)

    barrier = pltpu.get_barrier_semaphore()
    peers = [at_z(e) for e in SIGNS] + [at_quad(m) for m in (1, 2, 3)] + [at_xy(a, d) for a in ("x", "y") for d in SIGNS]
    for peer in peers:
        pl.semaphore_signal(barrier, inc=1, device_id=peer, device_id_type=MESH)
    k_me, _ = place("x", 0, 0)
    pairs = ((w3_hbm, w3), (tokens_hbm, tok.at[k_me, r]), (gout_hbm, gout), (sf_hbm, sf), (lf_hbm, lf))
    loads = [pltpu.make_async_copy(source, target, insem.at[n]) for n, (source, target) in enumerate(pairs)]
    for load in loads:
        load.start()
    before[...] = jnp.zeros_like(before)
    after[...] = jnp.zeros_like(after)
    loads[0].wait()
    for q in range(4):
        for i in range(3):
            wst[q, :, i * 128 : (i + 1) * 128] = w3[i, :, q * 128 : (q + 1) * 128]
    for i in range(3):
        wb[z, r, :, i * 128 : (i + 1) * 128] = w3[i, :, lanes(r)]
    for load in loads[1:]:
        load.wait()
    go[r] = gout[:, lanes(r)]
    sfs[...] = jnp.zeros_like(sfs)
    pl.semaphore_wait(barrier, len(peers))

    assert sorted(ORDER) == list(range(len(tasks)))
    order = [tasks[n] for n in ORDER]
    finished, started_sends = set(), set()
    for step in order:
        assert all(dep in finished or dep in started_sends for dep in step["deps"])
        finished.add(step["name"])
        started_sends.update(step["sends"])
    waited = set()
    for step in order:
        for dep in step["deps"]:
            if dep in msgs and dep not in waited:
                copy_of(dep).wait_recv()
                waited.add(dep)
        if step["run"] is not None:
            step["run"]()
        for name in step["sends"]:
            copy_of(name).start()
    for name in msgs:
        if name not in sent:
            copy_of(name).wait_send()


def scratch(nz, rows, cols, n_messages):
    ntok = 4 * rows
    quarter = rows // 4
    v = pltpu.VMEM
    return [
        v((3, 128, cols), BF16),
        v((3, 3, cols), F32),
        v((32, 128), BF16),
        v((rows, cols), BF16),
        v((nz, 4, rows, cols), BF16),
        v((4, 128, 384), BF16),
        v((nz, 4, 128, 384), BF16),
        v((4, rows, 128), BF16),
        v((ntok, 384), F32),
        v((256, 384), BF16),
        v((256, 384), BF16),
        v((2, 144, 384), BF16),
        v((3, 8, 16, ntok + 512), BF16),
        v((8, 16, ntok + 256), BF16),
        v((8, 256, 128), BF16),
        v((8, 128, 256), BF16),
        v((4, 8, 128), F32),
        v((128, 128), F32),
        v((8, 16, ntok), BF16),
        v((ntok, 128), BF16),
        v((4, rows, 128), BF16),
        v((3, 8, 16, ntok), BF16),
        v((ntok, 384), BF16),
        v((8, 16, ntok), BF16),
        v((8, 16, ntok + 512), BF16),
        v((3, 8, 16, ntok), F32),
        v((8, 128), F32),
        v((128, 128), F32),
        v((24, 128), F32),
        v((32, 128), BF16),
        v((nz - 1, 32, 128), BF16),
        v((24, 128), F32),
        v((3, 24, 128), F32),
        v((nz, 4, 384, 128), F32),
        v((4 * (nz - 1), 384, 128), BF16),
        v((4 * (nz - 1), 384, 128), BF16),
        v((3, 384, 128), BF16),
        v((3, 384, 128), BF16),
        v((8, 4, rows, cols), BF16),
        v((8, 2, rows, cols), BF16),
        v((2, 4, 2, quarter, cols), BF16),
        v((2, 4, 2, 2 * quarter, cols), BF16),
        v((2, 4, 2, 2 * quarter, cols), BF16),
        v((2, 4, 2 * quarter, cols), BF16),
        v((2, 2, quarter, cols), BF16),
        v((2, 2, 2 * quarter, cols), BF16),
        v((2, 2, 2 * quarter, cols), BF16),
        pltpu.SemaphoreType.DMA((n_messages,)),
        pltpu.SemaphoreType.DMA((n_messages,)),
        pltpu.SemaphoreType.DMA((5,)),
    ]


def per_device(tokens, in_weight, short_filter, long_filter, grad_out):
    rows, cols = tokens.shape
    nz = lax.axis_size("dp") // 4
    scale = float(rows * 4 * nz) ** (-0.5)
    vmem = pl.BlockSpec(memory_space=pltpu.VMEM)

    def body(*refs):
        block_kernel(*refs, nz=nz, scale=scale)

    results = pl.pallas_call(
        body,
        out_shape=(
            pltpu.VMEM((rows, cols), BF16),
            pltpu.VMEM((rows, cols), BF16),
            pltpu.VMEM((3, 128, cols), F32),
            pltpu.VMEM((32, 128), F32),
            pltpu.VMEM((3, 3, cols), F32),
        ),
        in_specs=[pl.BlockSpec(memory_space=pl.ANY)] * 5,
        out_specs=(vmem,) * 5,
        scratch_shapes=scratch(nz, rows, cols, 256),
        compiler_params=pltpu.CompilerParams(
            collective_id=0, has_side_effects=True, vmem_limit_bytes=62 * 1024 * 1024
        ),
        name="hyena_block",
    )(tokens, in_weight.transpose(1, 0, 2), short_filter, long_filter, grad_out)

    def hand_over(*refs):
        sems = refs[-1]
        copies = [pltpu.make_async_copy(a, b, sems.at[n]) for n, (a, b) in enumerate(zip(refs[:5], refs[5:10]))]
        for copy in copies:
            copy.start()
        for copy in copies:
            copy.wait()

    mixed, grad_in, grad_w, grad_long, grad_short = pl.pallas_call(
        hand_over,
        out_shape=tuple(jax.ShapeDtypeStruct(a.shape, a.dtype) for a in results),
        in_specs=[vmem] * 5,
        out_specs=(pl.BlockSpec(memory_space=pl.ANY),) * 5,
        scratch_shapes=[pltpu.SemaphoreType.DMA((5,))],
        name="hand_over",
    )(*[pltpu.with_memory_space_constraint(a, pltpu.VMEM) for a in results])
    return mixed, grad_in, grad_w.transpose(1, 0, 2), grad_long, grad_short


def solution(mesh):
    placed = (
        P("dp", ("row", "col")),
        P("dp", None, ("row", "col")),
        P(None, None, ("row", "col")),
        P(("row", "col"), None),
        P("dp", ("row", "col")),
    )
    return jax.shard_map(
        per_device,
        mesh=mesh,
        in_specs=placed,
        out_specs=(
            P("dp", ("row", "col")),
            P("dp", ("row", "col")),
            P("dp", None, ("row", "col")),
            P(("row", "col"), None),
            P(None, None, ("row", "col")),
        ),
        check_vma=False,
    )
```

```python
import jax
import jax.numpy as jnp
from jax import lax
from jax.experimental import pallas as pl
from jax.experimental.pallas import tpu as pltpu
from jax.sharding import PartitionSpec as P

MESH = pl.DeviceIdType.MESH
F32, BF16 = jnp.float32, jnp.bfloat16
SIGNS = (1, -1)
UNROLL = 1

ORDER = (
    30, 2, 6, 0, 33, 67, 61, 64, 92, 110, 13, 9, 32, 40, 43, 50, 34, 38, 37, 35, 7, 47, 31, 3,
    36, 78, 62, 81, 63, 71, 74, 14, 16, 19, 10, 44, 42, 41, 45, 39, 8, 23, 26, 4, 1, 66, 68, 69,
    65, 54, 57, 48, 49, 52, 15, 17, 51, 85, 88, 80, 82, 79, 83, 46, 20, 11, 75, 76, 73, 72, 59, 56,
    55, 58, 24, 53, 27, 5, 70, 60, 111, 18, 87, 86, 90, 89, 84, 21, 12, 77, 91, 28, 25, 93, 105, 107,
    94, 22, 103, 95, 104, 29, 96, 101, 100, 102, 98, 106, 99, 108, 97, 109, 112, 113, 114, 115, 127, 125, 151, 130,
    148, 131, 120, 141, 176, 144, 117, 119, 135, 129, 152, 149, 118, 133, 177, 142, 145, 189, 132, 128, 178, 218, 210, 150,
    216, 153, 195, 193, 190, 231, 181, 143, 146, 137, 179, 233, 126, 182, 223, 155, 154, 162, 221, 185, 180, 205, 200, 203,
    217, 219, 198, 147, 159, 166, 194, 139, 186, 228, 226, 134, 156, 116, 121, 174, 183, 220, 172, 163, 136, 196, 187, 157,
    184, 199, 222, 204, 224, 160, 191, 188, 206, 229, 167, 227, 197, 164, 201, 138, 192, 232, 234, 140, 208, 225, 236, 158,
    161, 173, 211, 122, 207, 124, 230, 237, 165, 168, 209, 239, 214, 202, 213, 175, 170, 235, 171, 169, 212, 123, 238, 215,
)


def block_kernel(
    tokens_hbm, w3_hbm, sf_hbm, lf_hbm, gout_hbm, mixed_out, gin_out, gw_out, gl_out, gs_out,
    w3, sf, lf, gout, tok, wst, wb, go, acc, before, after, edge, mx, gox, toe, voe, lfs, sfs, mxo, mxt, mr, gmt, gm,
    gcs, pds, gfs, glb, gsb, own_sums, smv, smr, smt, sqr, gp, ws, wr, fs, fr, pp, pr, q1, h1s, h1, s1, q2, h2s, h2,
    ssem, rsem, insem, *, nz, scale,
):
    dp, y, xl = lax.axis_index("dp"), lax.axis_index("row"), lax.axis_index("col")
    z, r = dp // 4, dp % 4
    xh, c = r // 2, r % 2
    x = xh * 2 + xl
    rows, cols = gout.shape
    quarter = rows // 4
    ntok = 4 * rows
    ngroups, members = mx.shape[1], mx.shape[2]
    nblocks = ntok // 128
    half_z = nz // 2

    def wrap(value, n):
        return lax.rem(value + 2 * n, n)

    def mate(m):
        other_h = 1 - xh if m & 2 else xh
        other_c = 1 - c if m & 1 else c
        return other_h * 2 + other_c

    def at_z(e):
        return (wrap(z + e, nz) * 4 + r, y, xl)

    def at_quad(m):
        return (z * 4 + mate(m), y, xl)

    def at_xy(axis, d):
        if axis == "y":
            return (dp, wrap(y + d, 4), xl)
        there = wrap(x + d, 4)
        return (z * 4 + (there // 2) * 2 + c, y, there % 2)

    def place(axis, first, second):
        dx, dy = (first, second) if axis == "x" else (second, first)
        px, py = wrap(x + dx, 4), wrap(y + dy, 4)
        return py * 2 + px % 2, px // 2

    msgs, tasks = {}, []

    def msg(name, src, dst, dev, link, nbytes, hops=1):
        msgs[name] = dict(src=src, dst=dst, dev=dev, link=link, bytes=nbytes, hops=hops, index=len(msgs))
        return name

    def task(name, deps=(), run=None, sends=(), cost=0.02, prio=5):
        tasks.append(dict(name=name, deps=list(deps), run=run, sends=list(sends), cost=cost, prio=prio))
        return name

    def copy_of(name):
        m = msgs[name]
        i = m["index"]
        return pltpu.make_async_remote_copy(
            src_ref=m["src"](), dst_ref=m["dst"](), send_sem=ssem.at[i], recv_sem=rsem.at[i],
            device_id=m["dev"](), device_id_type=MESH,
        )

    def lanes(block):
        return pl.ds(pl.multiple_of(block * 128, 128), 128)

    wbytes = 128 * 384 * 2
    for m in (1, 2, 3):
        link, hops = ("d", 1) if m == 1 else ("x2", 2)
        msg(("wq", m), lambda m=m: wst.at[mate(m)], lambda: wb.at[z, r], lambda m=m: at_quad(m), link, wbytes, hops)
        msg(("goq", m), lambda m=m: gout.at[:, lanes(mate(m))], lambda: go.at[r], lambda m=m: at_quad(m), link, rows * 256, hops)
    task("quad_w", sends=[("wq", 1), ("wq", 2), ("wq", 3)], prio=0)
    task("quad_go", deps=["quad_w", ("t2", 1, 0, 1)], sends=[("goq", 1), ("goq", 2), ("goq", 3)], prio=4)

    def reach(m, d):
        return half_z if (m < 2) == (d > 0) else half_z - 1

    for m in range(4):
        for d in SIGNS:
            for h in range(1, reach(m, d) + 1):
                where = lambda m=m, d=d, h=h: wb.at[wrap(z - d * (h - 1), nz), mate(m)]
                name = msg(("w", m, d, h), where, where, lambda d=d: at_z(d), "z+" if d > 0 else "z-", wbytes)
                if h > 1:
                    deps = [("w", m, d, h - 1)]
                else:
                    deps = [("wq", m)] if m else []
                task(("send", name), deps=deps, sends=[name], prio=0 if m < 2 else 1)

    hb, qb = 2 * quarter * cols * 2, quarter * cols * 2
    token_msgs = []
    for h in (0, 1):
        a1, a2 = ("x", "y") if h == 0 else ("y", "x")

        def piece(o, u, part, h=h, a1=a1):
            k, ph = place(a1, o, u)
            begin, size = {0: (0, 2), 1: (0, 1), -1: (1, 1)}[part]
            return tok.at[k, ph * 2 + c, pl.ds(h * 2 * quarter + begin * quarter, size * quarter), :]

        for d in SIGNS:
            w = lambda piece=piece: piece(0, 0, 0)
            msg(("t1", h, d), w, w, lambda a1=a1, d=d: at_xy(a1, d), a1 + "+-"[d < 0], hb)
            w = lambda piece=piece, d=d: piece(-d, 0, d)
            msg(("t1q", h, d), w, w, lambda a1=a1, d=d: at_xy(a1, d), a1 + "+-"[d < 0], qb)
            for o in (0, -1, 1, 2):
                w = lambda piece=piece, o=o: piece(o, 0, 0)
                msg(("t2", h, o, d), w, w, lambda a2=a2, d=d: at_xy(a2, d), a2 + "+-"[d < 0], hb)
                w = lambda piece=piece, o=o, d=d: piece(o, -d, d)
                msg(("t2q", h, o, d), w, w, lambda a2=a2, d=d: at_xy(a2, d), a2 + "+-"[d < 0], qb)
                token_msgs += [("t2", h, o, d), ("t2q", h, o, d)]
            token_msgs += [("t1", h, d), ("t1q", h, d)]
        for o in (0, -1, 1, 2):
            for u in (0, -1, 1, 2):
                w = lambda piece=piece, o=o, u=u: piece(o, u, 0)
                msg(("td", h, o, u), w, w, lambda: at_quad(1), "d", hb)
                token_msgs.append(("td", h, o, u))
        have = {0: [], -1: [("t1", h, 1)], 1: [("t1", h, -1)], 2: [("t1q", h, 1), ("t1q", h, -1)]}
        task(("tok1", h), deps=[], sends=[("t1", h, 1), ("t1", h, -1)], prio=0)
        for d in SIGNS:
            task(("tok1q", h, d), deps=[("t1", h, d)], sends=[("t1q", h, d)], prio=1)
        for o in (0, -1, 1, 2):
            task(("tok2", h, o), deps=have[o] + [("tok1", h)], sends=[("t2", h, o, 1), ("t2", h, o, -1)], prio=2)
            for d in SIGNS:
                task(("tok2q", h, o, d), deps=[("t2", h, o, d)], sends=[("t2q", h, o, d)], prio=2)
            there = {0: have[o], -1: [("t2", h, o, 1)], 1: [("t2", h, o, -1)], 2: [("t2q", h, o, 1), ("t2q", h, o, -1)]}
            for u in (0, -1, 1, 2):
                task(("tokd", h, o, u), deps=there[u], sends=[("td", h, o, u)], prio=3)
    task("tok_first", deps=[("tok1", 0), ("tok1", 1)], prio=0)
    task("tok_all", deps=token_msgs, prio=4)

    started = []

    def first_matmul(e, far):
        zs = wrap(z - e, nz)
        hf = 1 - xh if far else xh

        lhs = tok[zs, :, :, pl.ds(pl.multiple_of(hf * 256, 256), 256)].reshape(ntok, 256)
        rhs = wb[zs, pl.ds(hf * 2, 2)].reshape(256, 384)
        out = jnp.dot(lhs, rhs, preferred_element_type=F32)
        acc[...] = out + acc[...] if started else out
        started.append(e)

    mm = []
    for far in (False, True):
        for e in range(-half_z + 1, half_z + 1):
            pair = (2, 3) if far else (0, 1)
            if e == 0:
                deps = [("wq", m) for m in pair if m]
            elif e == half_z:
                d = -1 if far else 1
                deps = [("w", m, d, half_z) for m in pair]
            else:
                deps = [("w", m, 1 if e > 0 else -1, abs(e)) for m in pair]
            mm.append(task(("mm", e, far), deps=["tok_all"] + deps, run=lambda e=e, far=far: first_matmul(e, far), cost=0.45, prio=6))

    def build_toeplitz():
        for q in range(4):
            lfs[q] = lf[q * ngroups : (q + 1) * ngroups, :].astype(F32)
        for j in range(3):
            sfs[3 * j : 3 * j + 3, :] = sf[j, :, lanes(r)]

        def one(g, carry):
            row = lfs[r, pl.ds(g, 1), :]
            line = jnp.concatenate([row, jnp.zeros_like(row)], axis=1)
            skew = pltpu.roll(jnp.broadcast_to(line, (256, 256)), 0, 1, stride=1, stride_axis=0).astype(BF16)
            toe[g, 0:128, :] = skew[128:256, 0:128]
            toe[g, 128:256, :] = skew[0:128, 0:128]
            voe[g] = skew[0:128, :]
            return carry

        lax.fori_loop(0, ngroups, one, 0)
        sfs[...] = sfs[...].T

    task("toe", run=build_toeplitz, cost=3.0, prio=8)

    def turn_gout():
        flat = go[...].reshape(ntok, 128).T
        gox[:, :, 0:ntok] = flat.reshape(ngroups, members, ntok)

    msg(("goh",), lambda: gox.at[:, :, pl.ds(0, 256)], lambda: gox.at[:, :, pl.ds(ntok, 256)], lambda: at_z(-1), "z-", 128 * 512)
    task("got", deps=[("goq", 1), ("goq", 2), ("goq", 3)], run=turn_gout, sends=[("goh",)], cost=0.3, prio=3)

    def edge_rows():
        edge[0] = acc[0:144, :].astype(BF16)
        edge[1] = acc[ntok - 144 : ntok, :].astype(BF16)

    key, first = pl.ds(128, 256), pl.ds(0, 128)
    msg(("mh", 1, 1), lambda: edge.at[1, :, key], lambda: before.at[pl.ds(112, 144), key], lambda: at_z(1), "z+", 144 * 512)
    msg(("mh", 1, 0), lambda: edge.at[1, pl.ds(128, 16), first], lambda: before.at[pl.ds(240, 16), first], lambda: at_z(1), "z+", 16 * 256)
    msg(("mh", -1, 0), lambda: edge.at[0, :, first], lambda: after.at[pl.ds(0, 144), first], lambda: at_z(-1), "z-", 144 * 256)
    msg(("mh", -1, 1), lambda: edge.at[0, pl.ds(0, 16), key], lambda: after.at[pl.ds(0, 16), key], lambda: at_z(-1), "z-", 16 * 512)
    halos = [("mh", 1, 1), ("mh", 1, 0), ("mh", -1, 0), ("mh", -1, 1)]
    task("edge", deps=mm, run=edge_rows, sends=halos, cost=0.1, prio=0)

    def turn_mixed():
        for i in range(3):
            flat = acc[:, i * 128 : (i + 1) * 128].astype(BF16).T
            mx[i, :, :, 256 : 256 + ntok] = flat.reshape(ngroups, members, ntok)

    task("mxt", deps=["edge"], run=turn_mixed, cost=0.4, prio=0)

    def turn_halos():
        for i in range(3):
            for buf, off, dead in ((before, 0, z == 0), (after, 256 + ntok, z == nz - 1)):
                flat = buf[:, i * 128 : (i + 1) * 128].T
                mx[i, :, :, off : off + 256] = jnp.where(dead, jnp.zeros_like(flat), flat).reshape(ngroups, members, 256)
        ahead = gox[:, :, ntok : ntok + 256]
        gox[:, :, ntok : ntok + 256] = jnp.where(z == nz - 1, jnp.zeros_like(ahead), ahead)

    task("halo", deps=halos + [("goh",), "mxt", "got"], run=turn_halos, cost=0.3, prio=0)

    span = ntok + 128

    def tap_of(g):
        taps = sfs[pl.ds(pl.multiple_of(g * members, members), members), :]
        return lambda j, i: taps[:, 3 * j + i : 3 * j + i + 1]

    def local_operator():
        def group(g, carry):
            tap = tap_of(g)
            feats = []
            for i in range(3):
                base = mx[i, g].astype(F32)
                feats.append(tap(0, i) * base + tap(1, i) * pltpu.roll(base, 1, 1) + tap(2, i) * pltpu.roll(base, 2, 1))
            product = (feats[1] * feats[2]).astype(BF16)
            pds[g] = product
            windows = jnp.concatenate([product[:, 128 * (b + 1) : 128 * (b + 3)] for b in range(nblocks + 1)], axis=0)
            out = jnp.dot(windows, toe[g], preferred_element_type=F32)
            conv = jnp.concatenate([out[members * b : members * (b + 1)] for b in range(nblocks + 1)], axis=1)
            up = gox[g].astype(F32)
            query = feats[0][:, 256:]
            gconv = (up * query).astype(BF16)
            gcs[g] = gconv[:, :ntok]
            ahead = jnp.concatenate([gconv[:, 128 * b : 128 * (b + 2)] for b in range(nblocks + 1)], axis=0)
            back = lax.dot_general(ahead, voe[g], (((1,), (1,)), ((), ())), preferred_element_type=F32)
            gproduct = jnp.concatenate([back[members * b : members * (b + 1)] for b in range(nblocks + 1)], axis=1)
            mxo[g] = (query[:, :ntok] * conv[:, :ntok]).astype(BF16)
            gfeats = [
                up[:, :span] * conv,
                gproduct * feats[2][:, 256 : 256 + span],
                gproduct * feats[1][:, 256 : 256 + span],
            ]
            for i in range(3):
                grad = tap(0, i) * gfeats[i] + tap(1, i) * pltpu.roll(gfeats[i], span - 1, 1) + tap(2, i) * pltpu.roll(gfeats[i], span - 2, 1)
                gmt[i, g] = grad[:, :ntok].astype(BF16)
                gfs[i, g] = gfeats[i][:, :ntok]
            return carry

        lax.fori_loop(0, ngroups, group, 0, unroll=UNROLL)

    task("local", deps=["halo", "toe"], run=local_operator, cost=4.5, prio=0)

    def flip_matrix():
        turned = lax.broadcasted_iota(jnp.int32, (128, 128), 0) + lax.broadcasted_iota(jnp.int32, (128, 128), 1) == 127
        return turned.astype(F32).astype(BF16)

    def filter_sums(part, size):
        lane = lax.broadcasted_iota(jnp.int32, (members, 128), 1)
        flip = flip_matrix()

        def group(n, carry):
            g = part * size + n
            sums = jnp.zeros((members, 128), F32)
            for i in range(3):
                base = mx[i, g, :, 128 : 256 + ntok].astype(F32)
                for j in range(3):
                    late = pltpu.roll(base, j, 1) if j else base
                    both = gfs[i, g] * late[:, 128:]
                    total = both[:, 0:128]
                    for b in range(1, nblocks):
                        total = total + both[:, 128 * b : 128 * (b + 1)]
                    sums = jnp.where(lane == 3 * j + i, jnp.sum(total, axis=1, keepdims=True), sums)
            gsb[pl.ds(pl.multiple_of(g * members, members), members), :] = sums
            windows = jnp.concatenate([pds[g, :, 128 * (b + 1) : 128 * (b + 3)] for b in range(nblocks)], axis=0)
            held = jnp.concatenate([gcs[g, :, 128 * b : 128 * (b + 1)] for b in range(nblocks)], axis=0)
            flipped = jnp.dot(held, flip, preferred_element_type=F32).astype(BF16)
            pairs = lax.dot_general(flipped, windows, (((0,), (0,)), ((), ())), preferred_element_type=F32)
            skew = pltpu.roll(pairs, 0, 1, stride=1, stride_axis=0)
            glb[pl.ds(g, 1), :] = jnp.sum(skew, axis=0, keepdims=True)[:, 128:]
            return carry

        lax.fori_loop(0, size, group, 0)

    def filter_pack():
        own_sums[0:8, :] = jnp.dot(glb[...].astype(BF16), flip_matrix(), preferred_element_type=F32)
        own_sums[8:24, :] = gsb[...].T[0:16, :]
        smv[...] = jnp.concatenate([own_sums[...], jnp.zeros((8, 128), F32)], axis=0).astype(BF16)

    parts = 4
    for n in range(parts):
        task(("sums", n), deps=["local"], run=lambda n=n: filter_sums(n, ngroups // parts), cost=0.8, prio=(3.21, 3.22, 3.28, 3.29)[n])

    for m in (1, 2, 3):
        link, hops = ("d", 1) if m == 1 else ("x2", 2)
        msg(
            ("mq", m), lambda m=m: mxt.at[pl.ds(pl.multiple_of(mate(m) * rows, rows), rows), :], lambda: mr.at[r],
            lambda m=m: at_quad(m), link, rows * 256, hops,
        )
        msg(("sq", m), lambda: smt, lambda m=m: sqr.at[m - 1], lambda m=m: at_quad(m), link, 24 * 512, hops)

    def turn_output():
        for g in range(ngroups):
            mxt[:, g * members : (g + 1) * members] = mxo[g].T

    task("mixed_send", deps=["local"], run=turn_output, sends=[("mq", m) for m in (1, 2, 3)], cost=0.3, prio=3.34)
    offsets = [e for e in range(-half_z + 1, half_z + 1) if e]
    for n, e in enumerate(offsets):
        msg(("sm", e), lambda: smv, lambda n=n: smr.at[n], lambda e=e: at_z(e), "z+" if e > 0 else "z-", 32 * 256, abs(e))
    task("small_send", deps=[("sums", n) for n in range(parts)], run=filter_pack, sends=[("sm", e) for e in offsets], cost=0.1, prio=3.295)

    def small_total():
        total = own_sums[...]
        for n in range(len(offsets)):
            total = total + smr[n, 0:24].astype(F32)
        smt[...] = total * scale

    task("small", deps=[("sm", e) for e in offsets] + ["small_send"], run=small_total, sends=[("sq", m) for m in (1, 2, 3)], cost=0.1, prio=1)

    def small_out():
        for m in range(4):
            part = smt[...] if m == 0 else sqr[m - 1]
            q = mate(m)
            gl_out[pl.ds(pl.multiple_of(q * 8, 8), 8), :] = part[0:8]
            for j in range(3):
                gs_out[j, :, lanes(q)] = part[8 + 3 * j : 11 + 3 * j]

    task("small_out", deps=[("sq", m) for m in (1, 2, 3)] + ["small"], run=small_out, cost=0.1, prio=9)

    def mixed_final():
        mixed_out[:, lanes(r)] = mxt[pl.ds(pl.multiple_of(r * rows, rows), rows), :]
        for m in (1, 2, 3):
            mixed_out[:, lanes(mate(m))] = mr[mate(m)]

    task("mixed_out", deps=[("mq", m) for m in (1, 2, 3)] + ["mixed_send"], run=mixed_final, cost=0.1, prio=9)

    def weight_partial(e, far):
        zc = wrap(z + e, nz)
        hf = 1 - xh if far else xh
        rhs = tok[zc, :, :, pl.ds(pl.multiple_of(hf * 256, 256), 256)].reshape(ntok, 256)
        out = jnp.dot(gmt[...].reshape(384, ntok), rhs, preferred_element_type=F32)
        for n in range(2):
            gp[e % nz, hf * 2 + n] = out[:, n * 128 : (n + 1) * 128]

    chunks = [half_z]
    for e in range(half_z - 1, 0, -1):
        chunks += [e, -e]
    chunks.append(0)
    for n, e in enumerate(chunks):
        for far in (True, False):
            task(
                ("gw", e % nz, far), deps=["local"], run=lambda e=e, far=far: weight_partial(e, far), cost=0.38,
                prio=3 + 0.05 * n + (0 if far else 0.02),
            )
    slot = {}
    for m in range(4):
        for d in SIGNS:
            top = reach(m, d)
            for h in range(top, 0, -1):
                slot[m, d, h] = len(slot)
    for m in (2, 3, 1, 0):
        for d in SIGNS:
            top = reach(m, d)
            for h in range(top, 0, -1):
                s = slot[m, d, h]
                name = msg(("wr", m, d, h), lambda s=s: ws.at[s], lambda s=s: wr.at[s], lambda d=d: at_z(d), "z+" if d > 0 else "z-", wbytes)
                deps = [("gw", (d * h) % nz, m >= 2)]
                if h < top:
                    deps.append(("wr", m, d, h + 1))
                elif m < 2:
                    deps += [("send", "wr", 2, d, 1), ("send", "wr", 3, d, 1)]

                def add(m=m, d=d, h=h, s=s, top=top):
                    value = gp[(d * h) % nz, mate(m)]
                    if h < top:
                        value = value + wr[slot[m, d, h + 1]].astype(F32)
                    ws[s] = value.astype(BF16)

                task(("send", "wr", m, d, h), deps=deps, run=add, sends=[name], cost=0.12, prio=0 if m >= 2 else 1)

    def weight_total(m):
        return (gp[0, mate(m)] + wr[slot[m, 1, 1]].astype(F32) + wr[slot[m, -1, 1]].astype(F32)) * scale

    def weight_store(m, value):
        for i in range(3):
            gw_out[i, :, lanes(mate(m))] = value[i * 128 : (i + 1) * 128, :].T

    for m in range(4):
        deps = [("gw", 0, m >= 2), ("wr", m, 1, 1), ("wr", m, -1, 1)]
        if m == 0:
            task("wtot0", deps=deps, run=lambda: weight_store(0, weight_total(0)), cost=0.5, prio=8)
            continue
        link, hops = ("d", 1) if m == 1 else ("x2", 2)
        msg(("wf", m), lambda m=m: fs.at[m - 1], lambda m=m: fr.at[m - 1], lambda m=m: at_quad(m), link, wbytes, hops)

        def finish(m=m):
            fs[m - 1] = weight_total(m).astype(BF16)

        task(("wtot", m), deps=deps, run=finish, sends=[("wf", m)], cost=0.2, prio=1)
        task(("wout", m), deps=[("wf", m)], run=lambda m=m: weight_store(m, fr[m - 1].astype(F32)), cost=0.5, prio=8)

    def feature_block(dy, dx):
        return wrap(y + dy, 4) * 2 + wrap(xl + dx, 2)

    def token_partial(dy, dx):
        k = feature_block(dy, dx)
        out = lax.dot_general(gm[...], wb[k].reshape(512, 384), (((1,), (1,)), ((), ())), preferred_element_type=F32)
        pp[k] = out.astype(BF16).reshape(4, rows, cols)

    def pair_sum(dy, dx):
        k = feature_block(dy, dx)
        for ph in range(2):
            pp[k, ph * 2 + c] = (pp[k, ph * 2 + c].astype(F32) + pr[k, ph].astype(F32)).astype(BF16)

    def turn_grad():
        for i in range(3):
            gm[:, i * 128 : (i + 1) * 128] = gmt[i].reshape(128, ntok).T

    task("turn_grad", deps=["local"], run=turn_grad, cost=0.3, prio=3.155)
    for n, dy in enumerate((2, 1, -1, 0)):
        for dx in (0, 1):
            both = [
                msg(
                    ("pd", dy, dx, ph), lambda dy=dy, dx=dx, ph=ph: pp.at[feature_block(dy, dx), ph * 2 + (1 - c)],
                    lambda dy=dy, dx=dx, ph=ph: pr.at[feature_block(dy, dx), ph], lambda: at_quad(1), "d", rows * cols * 2,
                )
                for ph in range(2)
            ]
            task(("pk", dy, dx), deps=["turn_grad"], run=lambda dy=dy, dx=dx: token_partial(dy, dx), sends=both, cost=0.75, prio=(3.16, 3.27, 3.31, 3.36)[n] + 0.01 * dx)
            task(("pa", dy, dx), deps=both + [("pk", dy, dx)], run=lambda dy=dy, dx=dx: pair_sum(dy, dx), cost=0.25, prio=2.5)

    def part_rows(h, part):
        begin, size = {0: (0, 2), 1: (0, 1), -1: (1, 1)}[part]
        return pl.ds(h * 2 * quarter + begin * quarter, size * quarter)

    def own_rows(part):
        return slice(0, quarter) if part > 0 else slice(quarter, 2 * quarter)

    for h in (0, 1):
        a1, a2 = ("y", "x") if h == 0 else ("x", "y")

        def needs(o1, o2, h=h):
            dy, dx = (o1, o2) if h == 0 else (o2, o1)
            dy = {0: 0, 1: 1, -1: -1, 2: 2}[dy]
            return ("pa", dy, dx % 2)

        def held(o1, o2, part, h=h, a1=a1):
            k, ph = place(a1, o1, o2)
            return pp.at[k, ph * 2 + c, part_rows(h, part), :]

        for o in (2, 1, -1, 0):
            oi = o % 4
            for d in SIGNS:
                di = 0 if d > 0 else 1
                link1 = a1 + "+-"[d < 0]
                msg(("s1q", h, o, d), lambda held=held, o=o, d=d: held(2, o, d), lambda h=h, oi=oi, di=di: q1.at[h, oi, di], lambda a1=a1, d=d: at_xy(a1, d), link1, qb)
                msg(("s1h", h, o, d), lambda h=h, oi=oi, di=di: h1s.at[h, oi, di], lambda h=h, oi=oi, di=di: h1.at[h, oi, di], lambda a1=a1, d=d: at_xy(a1, d), link1, hb)
                task(("s1q", h, o, d, "go"), deps=[needs(2, o)], sends=[("s1q", h, o, d)], prio=1)

                def forward(h=h, o=o, oi=oi, d=d, di=di, held=held):
                    own = held(d, o, 0)[...]
                    mine, rest = own_rows(d), own_rows(-d)
                    h1s[h, oi, di, mine, :] = (own[mine].astype(F32) + q1[h, oi, di].astype(F32)).astype(BF16)
                    h1s[h, oi, di, rest, :] = own[rest]

                task(("s1h", h, o, d, "go"), deps=[("s1q", h, o, d), needs(d, o)], run=forward, sends=[("s1h", h, o, d)], cost=0.08, prio=2)

            def settle(h=h, o=o, oi=oi, held=held):
                total = held(0, o, 0)[...].astype(F32) + h1[h, oi, 0].astype(F32) + h1[h, oi, 1].astype(F32)
                s1[h, oi] = total.astype(BF16)

            sends = []
            if o == 2:
                for d in SIGNS:
                    di = 0 if d > 0 else 1
                    part = slice(0, quarter) if d > 0 else slice(quarter, 2 * quarter)
                    begin = 0 if d > 0 else quarter
                    sends.append(
                        msg(("s2q", h, d), lambda h=h, begin=begin: s1.at[h, 2, pl.ds(begin, quarter), :], lambda h=h, di=di: q2.at[h, di], lambda a2=a2, d=d: at_xy(a2, d), a2 + "+-"[d < 0], qb)
                    )
            task(("s1", h, o), deps=[("s1h", h, o, 1), ("s1h", h, o, -1), needs(0, o)], run=settle, sends=sends, cost=0.08, prio=2)
        for d in SIGNS:
            di = 0 if d > 0 else 1
            msg(("s2h", h, d), lambda h=h, di=di: h2s.at[h, di], lambda h=h, di=di: h2.at[h, di], lambda a2=a2, d=d: at_xy(a2, d), a2 + "+-"[d < 0], hb)

            def second(h=h, d=d, di=di):
                own = s1[h, d % 4]
                mine, rest = own_rows(d), own_rows(-d)
                h2s[h, di, mine, :] = (own[mine].astype(F32) + q2[h, di].astype(F32)).astype(BF16)
                h2s[h, di, rest, :] = own[rest]

            task(("s2h", h, d, "go"), deps=[("s2q", h, d), ("s1", h, d)], run=second, sends=[("s2h", h, d)], cost=0.08, prio=2)

        def last(h=h):
            total = s1[h, 0].astype(F32) + h2[h, 0].astype(F32) + h2[h, 1].astype(F32)
            gin_out[h * 2 * quarter : (h + 1) * 2 * quarter, :] = total.astype(BF16)

        task(("gin", h), deps=[("s2h", h, 1), ("s2h", h, -1), ("s1", h, 0)], run=last, cost=0.1, prio=8)

    sent = set()

    def drain(kinds):
        for name in msgs:
            if name not in sent and name[0] in kinds:
                copy_of(name).wait_send()
                sent.add(name)

    first_half = ("wq", "goq", "w", "t1", "t1q", "t2", "t2q", "td", "goh", "mh", "g")
    task("drain1", deps=["mixed_out"], run=lambda: drain(first_half), cost=0.6, prio=9)

    barrier = pltpu.get_barrier_semaphore()
    peers = [at_z(e) for e in SIGNS] + [at_quad(m) for m in (1, 2, 3)] + [at_xy(a, d) for a in ("x", "y") for d in SIGNS]
    for peer in peers:
        pl.semaphore_signal(barrier, inc=1, device_id=peer, device_id_type=MESH)
    k_me, _ = place("x", 0, 0)
    pairs = ((w3_hbm, w3), (tokens_hbm, tok.at[k_me, r]), (gout_hbm, gout), (sf_hbm, sf), (lf_hbm, lf))
    loads = [pltpu.make_async_copy(source, target, insem.at[n]) for n, (source, target) in enumerate(pairs)]
    for load in loads:
        load.start()
    before[...] = jnp.zeros_like(before)
    after[...] = jnp.zeros_like(after)
    loads[0].wait()
    for q in range(4):
        for i in range(3):
            wst[q, :, i * 128 : (i + 1) * 128] = w3[i, :, q * 128 : (q + 1) * 128]
    for i in range(3):
        wb[z, r, :, i * 128 : (i + 1) * 128] = w3[i, :, lanes(r)]
    for load in loads[1:]:
        load.wait()
    go[r] = gout[:, lanes(r)]
    sfs[...] = jnp.zeros_like(sfs)
    pl.semaphore_wait(barrier, len(peers))

    assert sorted(ORDER) == list(range(len(tasks)))
    order = [tasks[n] for n in ORDER]
    finished, started_sends = set(), set()
    for step in order:
        assert all(dep in finished or dep in started_sends for dep in step["deps"])
        finished.add(step["name"])
        started_sends.update(step["sends"])
    waited = set()
    launched = []
    for at, step in enumerate(order):
        if at in (len(order) - 24, len(order) - 12):
            for name in [n for n, begun in launched if begun < at - 24 and n not in sent]:
                copy_of(name).wait_send()
                sent.add(name)
        for dep in step["deps"]:
            if dep in msgs and dep not in waited:
                copy_of(dep).wait_recv()
                waited.add(dep)
        if step["run"] is not None:
            step["run"]()
        for name in step["sends"]:
            copy_of(name).start()
            launched.append((name, at))
    for name in msgs:
        if name not in sent:
            copy_of(name).wait_send()


def scratch(nz, rows, cols, n_messages):
    ntok = 4 * rows
    quarter = rows // 4
    v = pltpu.VMEM
    return [
        v((3, 128, cols), BF16),
        v((3, 3, cols), F32),
        v((32, 128), BF16),
        v((rows, cols), BF16),
        v((nz, 4, rows, cols), BF16),
        v((4, 128, 384), BF16),
        v((nz, 4, 128, 384), BF16),
        v((4, rows, 128), BF16),
        v((ntok, 384), F32),
        v((256, 384), BF16),
        v((256, 384), BF16),
        v((2, 144, 384), BF16),
        v((3, 8, 16, ntok + 512), BF16),
        v((8, 16, ntok + 256), BF16),
        v((8, 256, 128), BF16),
        v((8, 128, 256), BF16),
        v((4, 8, 128), F32),
        v((128, 128), F32),
        v((8, 16, ntok), BF16),
        v((ntok, 128), BF16),
        v((4, rows, 128), BF16),
        v((3, 8, 16, ntok), BF16),
        v((ntok, 384), BF16),
        v((8, 16, ntok), BF16),
        v((8, 16, ntok + 512), BF16),
        v((3, 8, 16, ntok), F32),
        v((8, 128), F32),
        v((128, 128), F32),
        v((24, 128), F32),
        v((32, 128), BF16),
        v((nz - 1, 32, 128), BF16),
        v((24, 128), F32),
        v((3, 24, 128), F32),
        v((nz, 4, 384, 128), F32),
        v((4 * (nz - 1), 384, 128), BF16),
        v((4 * (nz - 1), 384, 128), BF16),
        v((3, 384, 128), BF16),
        v((3, 384, 128), BF16),
        v((8, 4, rows, cols), BF16),
        v((8, 2, rows, cols), BF16),
        v((2, 4, 2, quarter, cols), BF16),
        v((2, 4, 2, 2 * quarter, cols), BF16),
        v((2, 4, 2, 2 * quarter, cols), BF16),
        v((2, 4, 2 * quarter, cols), BF16),
        v((2, 2, quarter, cols), BF16),
        v((2, 2, 2 * quarter, cols), BF16),
        v((2, 2, 2 * quarter, cols), BF16),
        pltpu.SemaphoreType.DMA((n_messages,)),
        pltpu.SemaphoreType.DMA((n_messages,)),
        pltpu.SemaphoreType.DMA((5,)),
    ]


def per_device(tokens, in_weight, short_filter, long_filter, grad_out):
    rows, cols = tokens.shape
    nz = lax.axis_size("dp") // 4
    scale = float(rows * 4 * nz) ** (-0.5)
    vmem = pl.BlockSpec(memory_space=pltpu.VMEM)

    def body(*refs):
        block_kernel(*refs, nz=nz, scale=scale)

    results = pl.pallas_call(
        body,
        out_shape=(
            pltpu.VMEM((rows, cols), BF16),
            pltpu.VMEM((rows, cols), BF16),
            pltpu.VMEM((3, 128, cols), F32),
            pltpu.VMEM((32, 128), F32),
            pltpu.VMEM((3, 3, cols), F32),
        ),
        in_specs=[pl.BlockSpec(memory_space=pl.ANY)] * 5,
        out_specs=(vmem,) * 5,
        scratch_shapes=scratch(nz, rows, cols, 256),
        compiler_params=pltpu.CompilerParams(
            collective_id=0, has_side_effects=True, vmem_limit_bytes=62 * 1024 * 1024
        ),
        name="hyena_block",
    )(tokens, in_weight.transpose(1, 0, 2), short_filter, long_filter, grad_out)

    def hand_over(*refs):
        sems = refs[-1]
        copies = [pltpu.make_async_copy(a, b, sems.at[n]) for n, (a, b) in enumerate(zip(refs[:5], refs[5:10]))]
        for copy in copies:
            copy.start()
        for copy in copies:
            copy.wait()

    mixed, grad_in, grad_w, grad_long, grad_short = pl.pallas_call(
        hand_over,
        out_shape=tuple(jax.ShapeDtypeStruct(a.shape, a.dtype) for a in results),
        in_specs=[vmem] * 5,
        out_specs=(pl.BlockSpec(memory_space=pl.ANY),) * 5,
        scratch_shapes=[pltpu.SemaphoreType.DMA((5,))],
        name="hand_over",
    )(*[pltpu.with_memory_space_constraint(a, pltpu.VMEM) for a in results])
    return mixed, grad_in, grad_w.transpose(1, 0, 2), grad_long, grad_short


def solution(mesh):
    placed = (
        P("dp", ("row", "col")),
        P("dp", None, ("row", "col")),
        P(None, None, ("row", "col")),
        P(("row", "col"), None),
        P("dp", ("row", "col")),
    )
    return jax.shard_map(
        per_device,
        mesh=mesh,
        in_specs=placed,
        out_specs=(
            P("dp", ("row", "col")),
            P("dp", ("row", "col")),
            P("dp", None, ("row", "col")),
            P(("row", "col"), None),
            P(None, None, ("row", "col")),
        ),
        check_vma=False,
    )
```
